1024 devices in a mesh: seq: 64 (over z, y_hi), fsdp: 8 (over x, core), canvas: 2 (over y_lo).
Axes of the slice: x: 4, y: 8 (y_hi: 4, y_lo: 2; y = y_hi * 2 + y_lo), z: 16, core: 2. Of those that a mesh axis runs over, the one named last changes fastest.
Arguments:
- patch_tokens: bfloat16 [8, 16384, 1024], P('fsdp', 'seq'), may hold values from -6 to 6
- keep_mask: int32 [8, 16384], P('fsdp', 'seq'), may hold values from 0 to 1, as said below
- slot_index: int32 [8, 16384], P('fsdp', 'seq'), may hold values from 0 to 8191, as said below
- tile_map: int32 [8, 1024], P('fsdp', 'seq'), may hold values from 0 to 1023, each once within a row
- qkv_proj: bfloat16 [1024, 2, 3, 512], P(None, 'canvas'), may hold values from -1 to 1
- out_proj: bfloat16 [1024, 1024], replicated, may hold values from -0.1875 to 0.1875
- up_proj: bfloat16 [1024, 4096], P('fsdp', 'canvas'), may hold values from -0.1875 to 0.1875
- down_proj: bfloat16 [1024, 4096], P('fsdp', 'canvas'), may hold values from -0.09375 to 0.09375
Outputs:
- encoded: bfloat16 [8, 8192, 1024], P('fsdp', ('seq', 'canvas'))
The draws below stay inside these ranges and needn't reach their ends.
Inputs may be any that keep to these rules, and one draw needn't show every extreme that they name: Exactly 8192 tokens of each scene have keep_mask 1. Over the kept tokens of a scene, slot_index takes every value below 8192 once. The kept tokens of one index of seq whose slots fall in one block of 128 slots fill one whole aligned run of 4 slots; each block is filled by runs from 32 indices of seq. `tile_map`: each canvas tile of a scene appears once.
All inputs are finite; a program needn't handle non-finite values.
Results may differ from the reference program's by a relative error of at most 0.0085.
Values may be sent and summed in bfloat16 or wider, within the bound.
A program may use at most 64 MiB of HBM per device.

```python
import jax
import jax.numpy as jnp
from jax import lax

D = 1024
HEADS = 16
HEAD_DIM = 64
FF = 4096
TILE_SIDE = 4
TILES_W = 32
VIS_DEV = 128
TOK_DEV = 256
VIS = 8192
SEQ_TOK = 16384
TILES = 1024
SCENES = 8
N_SEQ = 64
N_FSDP = 8
N_CANVAS = 2


def token_order(rank_key):
    return jax.random.permutation(rank_key, TOK_DEV).astype(jnp.int32)


def route_one(scene_key):
    run_length = 2 * VIS_DEV // N_SEQ
    groups = N_SEQ // 2
    busy_level = jax.random.randint(jax.random.fold_in(scene_key, 1), (N_SEQ,), 0, 4)
    noise_draw = jax.random.randint(jax.random.fold_in(scene_key, 2), (N_SEQ, N_SEQ), 0, 65536)
    sources = jnp.arange(N_SEQ, dtype=jnp.int32)
    pick_score = (busy_level[None, :] * 24576 + noise_draw) * N_SEQ + sources[None, :]
    picked = lax.top_k(pick_score, groups)[1].astype(jnp.int32)
    hit_table = (picked[:, :, None] == sources[None, None, :]).astype(jnp.int32)
    chosen = jnp.sum(hit_table, axis=1)
    group_of = jnp.sum(hit_table * jnp.arange(groups, dtype=jnp.int32)[None, :, None], axis=1)
    target_order = jnp.cumsum(chosen, axis=0) - 1
    kept_quota = run_length * jnp.sum(chosen, axis=0)
    rank_keys = jax.random.split(jax.random.fold_in(scene_key, 3), N_SEQ)
    token_rank = jax.vmap(token_order)(rank_keys)
    which_target = token_rank // run_length
    match_table = ((jnp.transpose(chosen)[:, None, :] == 1) & (jnp.transpose(target_order)[:, None, :] == which_target[:, :, None])).astype(jnp.int32)
    targets = jnp.sum(match_table * sources[None, None, :], axis=2)
    group_pos = jnp.sum(match_table * jnp.transpose(group_of)[:, None, :], axis=2)
    kept_here = token_rank < kept_quota[:, None]
    slot_kept = targets * VIS_DEV + group_pos * run_length + token_rank % run_length
    filler = jax.random.randint(jax.random.fold_in(scene_key, 4), (N_SEQ, TOK_DEV), 0, N_SEQ * VIS_DEV)
    slot_all = jnp.where(kept_here, slot_kept, filler).reshape(-1).astype(jnp.int32)
    return (kept_here.astype(jnp.int32).reshape(-1), slot_all)


def route_plan(key):
    scene_keys = jax.random.split(jax.random.fold_in(key, 11), N_FSDP)
    return jax.vmap(route_one)(scene_keys)


def draw_keep_mask(key, part):
    return route_plan(key)[0]


def draw_slot_index(key, part):
    return route_plan(key)[1]


def draw_patch_tokens(key, part):
    shape_all = (N_FSDP, SEQ_TOK, D)
    base_noise = jax.random.normal(jax.random.fold_in(key, 1), shape_all, jnp.float32)
    return jnp.clip(base_noise, -6.0, 6.0).astype(jnp.bfloat16)


def draw_qkv_proj(key, part):
    shape_all = (D, N_CANVAS, 3, D // N_CANVAS)
    weights = jnp.clip(jax.random.normal(jax.random.fold_in(key, 5), shape_all, jnp.float32), -6.0, 6.0) * D ** (-0.5)
    return weights.astype(jnp.bfloat16)


def levels(rng, extent, shards, low, largest):
    def one(position, blocks):
        steps = jax.random.uniform(jax.random.fold_in(jax.random.fold_in(rng, 6), position), (blocks,), jnp.float32, low / len(shards), largest / len(shards))
        return jnp.repeat(jnp.exp(steps), extent[position] // blocks).reshape((-1,) + (1,) * (len(extent) - position - 1))

    gain = one(*shards[0])
    for cut in shards[1:]:
        gain = gain * one(*cut)
    return gain


def scatter_about(rng, dims, scale, reach, pieces=(), held_as=jnp.bfloat16):
    drawn = scale * jax.random.normal(rng, dims, jnp.float32)
    if pieces:
        drawn = drawn * levels(rng, dims, pieces, -0.22, 0.18)
    return jnp.clip(drawn, -reach, reach).astype(held_as)


def setup_inputs(seed: int = 0) -> dict:
    streams_of = jax.random.split(jax.random.key(seed), 9)
    patch_tokens = draw_patch_tokens(jax.random.fold_in(streams_of[8], 71), 0)
    keep_mask = draw_keep_mask(jax.random.fold_in(streams_of[8], 71), 0)
    slot_index = draw_slot_index(jax.random.fold_in(streams_of[8], 71), 0)
    tile_map = jax.vmap(lambda own: jax.random.permutation(own, TILES))(jax.random.split(streams_of[3], SCENES)).reshape((SCENES, TILES)).astype(jnp.int32)
    qkv_proj = draw_qkv_proj(jax.random.fold_in(streams_of[8], 71), 0)
    out_proj = scatter_about(streams_of[5], (D, D), D ** -0.5, 0.1875)
    up_proj = scatter_about(streams_of[6], (D, FF), D ** -0.5, 0.1875, ((0, 8), (1, 2)))
    down_proj = scatter_about(streams_of[7], (D, FF), FF ** -0.5, 0.09375, ((0, 8), (1, 2)))
    return dict(patch_tokens=patch_tokens, keep_mask=keep_mask, slot_index=slot_index, tile_map=tile_map, qkv_proj=qkv_proj, out_proj=out_proj, up_proj=up_proj, down_proj=down_proj)


EPS = 1e-06

def layer_norm(values):
    centered = values - lax.optimization_barrier(jnp.mean(values, axis=-1, keepdims=True))
    spread = lax.optimization_barrier(jnp.mean(centered * centered, axis=-1, keepdims=True))
    return centered * lax.rsqrt(spread + EPS)

def position_table(tile_ids):
    tile_count = tile_ids.shape[0]
    tile_size = TILE_SIDE * TILE_SIDE
    tile_cell = jnp.repeat(tile_ids, tile_size)
    within = jnp.arange(tile_count * tile_size, dtype=jnp.int32) % tile_size
    row_at = tile_cell // TILES_W * TILE_SIDE + within // TILE_SIDE
    col_at = tile_cell % TILES_W * TILE_SIDE + within % TILE_SIDE
    quarter = D // 4
    frequency = 10000.0 ** (-jnp.arange(quarter, dtype=jnp.float32) / quarter)
    row_angle = row_at.astype(jnp.float32)[:, None] * frequency[None, :]
    col_angle = col_at.astype(jnp.float32)[:, None] * frequency[None, :]
    return jnp.concatenate([jnp.sin(row_angle), jnp.cos(row_angle), jnp.sin(col_angle), jnp.cos(col_angle)], axis=1)

def attend_block(inputs):
    query_blk, key_blk, value_blk, key_prev, value_prev = inputs
    keys_all = jnp.concatenate([key_blk, key_prev], axis=0).astype(jnp.float32)
    values_all = jnp.concatenate([value_blk, value_prev], axis=0).astype(jnp.float32)
    scores = jnp.einsum('qhe,khe->hqk', query_blk.astype(jnp.float32), keys_all) * HEAD_DIM ** (-0.5)
    row_peak = lax.optimization_barrier(jnp.max(scores, axis=-1, keepdims=True))
    expo_terms = jnp.exp(scores - row_peak)
    row_total = lax.optimization_barrier(jnp.sum(expo_terms, axis=-1))
    probs = lax.optimization_barrier(expo_terms.astype(jnp.bfloat16))
    summed = jnp.einsum('hqk,khe->qhe', probs.astype(jnp.float32), values_all)
    return (summed / jnp.transpose(row_total)[:, :, None]).astype(jnp.bfloat16)

def one_scene(inputs, qkv_proj, out_proj, up_proj, down_proj):
    patch_tokens, keep_mask, slot_index, tile_map = inputs
    embedded = (patch_tokens.astype(jnp.float32) + position_table(tile_map)).astype(jnp.bfloat16)
    target = jnp.where(keep_mask == 1, slot_index, VIS)
    visible = jnp.zeros((VIS, D), jnp.bfloat16).at[target].set(embedded, mode='drop')
    normed = layer_norm(visible.astype(jnp.float32)).astype(jnp.bfloat16)
    qkv = jnp.dot(normed, qkv_proj.reshape(D, 3 * D), preferred_element_type=jnp.float32).astype(jnp.bfloat16)
    qkv = qkv.reshape(VIS, N_CANVAS, 3, D // N_CANVAS)
    queries = qkv[:, :, 0, :].reshape(N_SEQ, VIS_DEV, HEADS, HEAD_DIM)
    keys_now = qkv[:, :, 1, :].reshape(N_SEQ, VIS_DEV, HEADS, HEAD_DIM)
    values_now = qkv[:, :, 2, :].reshape(N_SEQ, VIS_DEV, HEADS, HEAD_DIM)
    keys_prev = jnp.roll(keys_now, 1, axis=0)
    values_prev = jnp.roll(values_now, 1, axis=0)
    attended = lax.map(attend_block, (queries, keys_now, values_now, keys_prev, values_prev)).reshape(VIS, D)
    head_mixed = jnp.dot(attended, out_proj, preferred_element_type=jnp.float32)
    residual = visible.astype(jnp.float32) + head_mixed
    normed_two = layer_norm(residual).astype(jnp.bfloat16)
    hidden = jax.nn.gelu(jnp.dot(normed_two, up_proj, preferred_element_type=jnp.float32), approximate=False).astype(jnp.bfloat16)
    output_terms = jnp.dot(hidden, jnp.transpose(down_proj), preferred_element_type=jnp.float32)
    return (residual + output_terms).astype(jnp.bfloat16)

def reference(patch_tokens, keep_mask, slot_index, tile_map, qkv_proj, out_proj, up_proj, down_proj):

    def per_scene(inputs):
        return one_scene(inputs, qkv_proj, out_proj, up_proj, down_proj)
    return lax.map(per_scene, (patch_tokens, keep_mask, slot_index, tile_map))
```

```python
import functools

import jax
import jax.numpy as jnp
import numpy as np
from jax import lax
from jax.experimental import pallas as pl
from jax.experimental.pallas import tpu as pltpu
from jax.sharding import PartitionSpec as P

D = 1024
HALF = 512
QUART = 256
EPS = 1e-06
MESH = pl.DeviceIdType.MESH
F32 = jnp.float32
BF16 = jnp.bfloat16


def normalised(values):
    centered = values - jnp.mean(values, axis=-1, keepdims=True)
    spread = jnp.mean(centered * centered, axis=-1, keepdims=True)
    return centered * lax.rsqrt(spread + EPS)


def matmul(left, right):
    return jnp.dot(left, right, preferred_element_type=F32)


def matmul_nt(left, right):
    return lax.dot_general(left, right, (((1,), (1,)), ((), ())), preferred_element_type=F32)


def gelu(x):
    return 0.5 * x * (1.0 + lax.erf(x * (0.5**0.5)))


def kernel(
    n_seq, chunks,
    tile_ref, keep_ref, slot_ref, freq_ref, patch_hbm, qkv_hbm, out_hbm, up_hbm, down_hbm,
    y_ref,
    patch_v, qkv_v, out_v, up_v, down_v,
    emb, send, recv, lab_out, lab_in, vis, normed, q_s, k_s, v_s, att, resid, normed2, hidden, part, y_out, y_in,
    load_sem, a2a_sem, vis_ssem, vis_rsem, w_ssem, w_rsem, att_sem, y_ssem, y_rsem,
):
    s = lax.axis_index("seq")
    f = lax.axis_index("fsdp")
    c = lax.axis_index("canvas")
    other = 1 - c
    f_right, f_left, f_far = lax.rem(f + 2, 8), lax.rem(f + 6, 8), lax.rem(f + 4, 8)
    mate = f + 1 - 2 * lax.rem(f, 2)
    m_right, m_left, m_far = lax.rem(mate + 2, 8), lax.rem(mate + 6, 8), lax.rem(mate + 4, 8)
    s_next = lax.rem(s + 1, n_seq)
    s_diag = lax.rem(s + n_seq + 2 * c - 1, n_seq)

    barrier = pltpu.get_barrier_semaphore()

    def greet(i, carry):
        pl.semaphore_signal(barrier, inc=1, device_id={"seq": lax.rem(s + i, n_seq)}, device_id_type=MESH)
        return carry

    lax.fori_loop(1, n_seq, greet, 0)
    for peer in (f_right, f_left, mate):
        pl.semaphore_signal(barrier, inc=1, device_id={"fsdp": peer}, device_id_type=MESH)
    pl.semaphore_signal(barrier, inc=1, device_id={"canvas": other}, device_id_type=MESH)
    pl.semaphore_signal(barrier, inc=1, device_id={"seq": s_diag, "canvas": other}, device_id_type=MESH)

    col0 = pl.multiple_of(c * HALF, HALF)
    patch_load = pltpu.make_async_copy(patch_hbm.at[0, :, pl.ds(col0, HALF)], patch_v, load_sem.at[0])
    qkv_load = pltpu.make_async_copy(qkv_hbm, qkv_v, load_sem.at[1])
    out_load = pltpu.make_async_copy(out_hbm, out_v, load_sem.at[2])

    def rows_of(shard):
        return pl.ds(pl.multiple_of(shard * 128, 128), 128)

    up_load = pltpu.make_async_copy(up_hbm, up_v.at[rows_of(f)], load_sem.at[3])
    down_load = pltpu.make_async_copy(down_hbm, down_v.at[rows_of(f)], load_sem.at[4])
    for load in (patch_load, qkv_load, out_load, up_load, down_load):
        load.start()

    slot = slot_ref[...]
    kept = keep_ref[...] == 1
    target = slot // 128
    lane4 = lax.rem(slot, 4)
    group = lax.rem(slot, 128) // 4
    first = jnp.where(kept & (lane4 == 0), target, -1)
    group_val = jnp.broadcast_to((group + 1).astype(F32), (8, 256)).astype(BF16)
    t_rows = lax.broadcasted_iota(jnp.int32, (128, 256), 0)
    hit = jnp.where(t_rows == first, 1.0, 0.0).astype(BF16)
    labels = matmul_nt(group_val, hit)
    lab_out[...] = labels[0:1, :]

    patch_load.wait()
    freq = freq_ref[...]
    within = lax.broadcasted_iota(jnp.int32, (16, QUART), 0)
    cell = jnp.where(c == 0, within // 4, lax.rem(within, 4))

    def embed(t, carry):
        tile = tile_ref[0, t]
        base = jnp.where(c == 0, tile // 32, lax.rem(tile, 32)) * 4
        angle = (base + cell).astype(F32) * freq
        rows = pl.ds(pl.multiple_of(t * 16, 16), 16)
        emb[0, rows, :] = (patch_v[rows, 0:QUART].astype(F32) + jnp.sin(angle)).astype(BF16)
        emb[1, rows, :] = (patch_v[rows, QUART:HALF].astype(F32) + jnp.cos(angle)).astype(BF16)
        return carry

    lax.fori_loop(0, 16, embed, 0)

    key = jnp.where(kept, target * 4 + lane4, -1000)
    row_i = lax.broadcasted_iota(jnp.int32, (512, QUART), 0)
    row_key = row_i // 8 * 4 + lax.rem(row_i, 4) + lax.rem(row_i // 4, 2) * 256
    pick0 = jnp.where(row_key == key, 1.0, 0.0).astype(BF16)
    pick1 = jnp.where(row_key == key + 256, 1.0, 0.0).astype(BF16)
    packed = matmul(pick0, emb[0]) + matmul(pick1, emb[1])
    send[...] = packed.astype(BF16).reshape(n_seq, 8, QUART)

    pl.semaphore_wait(barrier, n_seq + 4)

    def push(i, carry):
        step = 32 + (i + 1) // 2 * (2 * lax.rem(i, 2) - 1)
        to = lax.rem(s + step, n_seq)
        pltpu.make_async_remote_copy(
            src_ref=lab_out, dst_ref=lab_in.at[s], send_sem=a2a_sem.at[0], recv_sem=a2a_sem.at[1],
            device_id={"seq": to}, device_id_type=MESH,
        ).start()
        pltpu.make_async_remote_copy(
            src_ref=send.at[to], dst_ref=recv.at[s], send_sem=a2a_sem.at[2], recv_sem=a2a_sem.at[3],
            device_id={"seq": to}, device_id_type=MESH,
        ).start()
        return carry

    lax.fori_loop(0, n_seq - 1, push, 0)
    own_label = pltpu.make_async_copy(lab_out, lab_in.at[s], a2a_sem.at[4])
    own_label.start()
    own_rows = pltpu.make_async_copy(send.at[s], recv.at[s], a2a_sem.at[5])
    own_rows.start()

    def ship(src, buf, shard, to, index_s, index_r):
        copy = pltpu.make_async_remote_copy(
            src_ref=src, dst_ref=buf.at[rows_of(shard)], send_sem=w_ssem.at[index_s], recv_sem=w_rsem.at[index_r],
            device_id={"fsdp": to}, device_id_type=MESH,
        )
        copy.start()
        return copy

    def landed(buf, shard, index_r):
        view = buf.at[rows_of(shard)]
        pltpu.make_async_copy(view, view, w_rsem.at[index_r]).wait()

    shipped = [
        ship(up_hbm, up_v, f, f_right, 0, 0),
        ship(down_hbm, down_v, f, f_left, 1, 3),
        ship(down_hbm, down_v, f, f_right, 2, 1),
        ship(up_hbm, up_v, f, f_left, 3, 2),
        ship(up_hbm, up_v, f, mate, 4, 6),
        ship(down_hbm, down_v, f, mate, 5, 7),
    ]

    own_label.wait()
    pltpu.make_async_copy(lab_in.at[pl.ds(0, n_seq - 1)], lab_in.at[pl.ds(0, n_seq - 1)], a2a_sem.at[1]).wait()
    lane_of = lax.broadcasted_iota(jnp.int32, (8, 128), 1)
    mine = jnp.where(lane_of == s, 1.0, 0.0).astype(BF16)
    came = matmul_nt(mine, lab_in[...].reshape(n_seq, 128).astype(BF16))
    spread_r = lax.broadcasted_iota(jnp.int32, (n_seq, 512), 0)
    spread_c = lax.broadcasted_iota(jnp.int32, (n_seq, 512), 1)
    spread = jnp.where(spread_r == spread_c // 8, 1.0, 0.0).astype(BF16)
    label_of = matmul(came.astype(BF16), spread).astype(jnp.int32)
    col_i = lax.broadcasted_iota(jnp.int32, (8, 512), 1)
    row_of = label_of * 4 - 4 + lax.rem(col_i, 4)
    half_of = lax.rem(col_i // 4, 2)
    r_i = lax.broadcasted_iota(jnp.int32, (128, 512), 0)
    places = []
    for h in range(2):
        row_h = jnp.where(half_of == h, row_of, -1)[0:1, :]
        places.append(jnp.where(r_i == row_h, 1.0, 0.0).astype(BF16))
    own_rows.wait()
    pltpu.make_async_copy(recv.at[pl.ds(0, n_seq - 1)], recv.at[pl.ds(0, n_seq - 1)], a2a_sem.at[3]).wait()
    came_rows = recv[...].reshape(512, QUART)
    for h in range(2):
        vis[0, c, :, h * QUART:(h + 1) * QUART] = matmul(places[h], came_rows).astype(BF16)

    size = 128 // chunks

    def view_of(block, half, k):
        return vis.at[block, half, pl.ds(k * size, size), :]

    def pass_on(half, src_block, dst_block, k, to, index_s, index_r):
        copy = pltpu.make_async_remote_copy(
            src_ref=view_of(src_block, half, k), dst_ref=view_of(dst_block, half, k),
            send_sem=vis_ssem.at[index_s * chunks + k], recv_sem=vis_rsem.at[index_r * chunks + k],
            device_id=to, device_id_type=MESH,
        )
        copy.start()
        return copy

    def arrived(block, half, k, index_r):
        view = view_of(block, half, k)
        pltpu.make_async_copy(view, view, vis_rsem.at[index_r * chunks + k]).wait()

    def sent(half, k, index_s):
        view = view_of(0, half, k)
        pltpu.make_async_copy(view, view, vis_ssem.at[index_s * chunks + k]).wait()

    pair = {"canvas": other}
    onward = {"seq": s_next, "canvas": 0}
    for k in range(chunks):
        pass_on(c, 0, 0, k, pair, 0, 0)

    @pl.when(c == 1)
    def _():
        for k in range(chunks):
            pass_on(1, 0, 1, k, onward, 1, 1)
        for k in range(chunks):
            arrived(0, 0, k, 0)
            pass_on(0, 0, 1, k, onward, 2, 2)

    @pl.when(c == 0)
    def _():
        for k in range(chunks):
            arrived(1, 1, k, 1)
            pass_on(1, 1, 1, k, pair, 1, 1)
        for k in range(chunks):
            arrived(0, 1, k, 0)

    landed(up_v, f_left, 0)
    shipped.append(ship(up_v.at[rows_of(f_left)], up_v, f_left, f_right, 6, 4))
    landed(down_v, f_right, 3)
    shipped.append(ship(down_v.at[rows_of(f_right)], down_v, f_right, f_left, 7, 5))
    shipped.append(ship(up_v.at[rows_of(f_left)], up_v, f_left, mate, 8, 8))
    shipped.append(ship(down_v.at[rows_of(f_right)], down_v, f_right, mate, 9, 11))

    qkv_load.wait()
    visible = jnp.concatenate([vis[0, 0], vis[0, 1]], axis=1).astype(F32)
    normed[...] = normalised(visible).astype(BF16)
    q_s[...] = matmul(normed[...], qkv_v[0]).astype(BF16)
    k_s[0:128, :] = matmul(normed[...], qkv_v[1]).astype(BF16)
    v_s[0:128, :] = matmul(normed[...], qkv_v[2]).astype(BF16)

    @pl.when(c == 0)
    def _():
        for k in range(chunks):
            arrived(1, 0, k, 2)
            pass_on(0, 1, 1, k, pair, 2, 2)

    @pl.when(c == 1)
    def _():
        for k in range(chunks):
            arrived(1, 1, k, 1)
        for k in range(chunks):
            arrived(1, 0, k, 2)

    before = jnp.concatenate([vis[1, 0], vis[1, 1]], axis=1).astype(F32)
    normed[...] = normalised(before).astype(BF16)
    k_s[128:256, :] = matmul(normed[...], qkv_v[1]).astype(BF16)
    v_s[128:256, :] = matmul(normed[...], qkv_v[2]).astype(BF16)

    low = lax.broadcasted_iota(jnp.int32, (128, 128), 1) < 64
    for p in range(4):
        lanes = pl.ds(p * 128, 128)
        q_pair, k_pair, v_pair = q_s[:, lanes], k_s[:, lanes], v_s[:, lanes]
        mixed = []
        for e in range(2):
            q_one = jnp.where(low == (e == 0), q_pair.astype(F32), 0.0).astype(BF16)
            scores = matmul_nt(q_one, k_pair) * 0.125
            expo = jnp.exp(scores - jnp.max(scores, axis=-1, keepdims=True))
            total = jnp.sum(expo, axis=-1, keepdims=True)
            mixed.append(matmul(expo.astype(BF16), v_pair) / total)
        att[c, :, lanes] = jnp.where(low, mixed[0], mixed[1]).astype(BF16)

    att_copy = pltpu.make_async_remote_copy(
        src_ref=att.at[c], dst_ref=att.at[c], send_sem=att_sem.at[0], recv_sem=att_sem.at[1],
        device_id=pair, device_id_type=MESH,
    )
    att_copy.start()

    landed(down_v, f_left, 1)
    shipped.append(ship(down_v.at[rows_of(f_left)], down_v, f_left, mate, 10, 9))
    landed(up_v, f_right, 2)
    shipped.append(ship(up_v.at[rows_of(f_right)], up_v, f_right, mate, 11, 10))

    out_load.wait()
    att_copy.wait_recv()
    mixed_in = jnp.concatenate([att[0], att[1]], axis=1)
    visible = jnp.concatenate([vis[0, 0], vis[0, 1]], axis=1).astype(F32)
    resid[...] = visible + matmul(mixed_in, out_v[...])
    normed2[...] = normalised(resid[...]).astype(BF16)

    landed(up_v, f_far, 4)
    shipped.append(ship(up_v.at[rows_of(f_far)], up_v, f_far, mate, 12, 12))
    landed(down_v, f_far, 5)
    shipped.append(ship(down_v.at[rows_of(f_far)], down_v, f_far, mate, 13, 13))

    up_load.wait()
    down_load.wait()
    landed(up_v, mate, 6)
    landed(up_v, m_left, 8)
    landed(up_v, m_right, 10)
    landed(up_v, m_far, 12)

    def widen(n, carry):
        cols = pl.ds(pl.multiple_of(n * 256, 256), 256)
        hidden[:, cols] = gelu(matmul(normed2[...], up_v[:, cols])).astype(BF16)
        return carry

    lax.fori_loop(0, 8, widen, 0)

    landed(down_v, mate, 7)
    landed(down_v, m_left, 9)
    landed(down_v, m_right, 11)
    landed(down_v, m_far, 13)

    here = pl.ds(pl.multiple_of(c * 64, 64), 64)
    there = pl.ds(pl.multiple_of(other * 64, 64), 64)
    y_copies = []
    for n in range(4):
        cols = pl.ds(n * 256, 256)
        part[:, cols] = matmul_nt(hidden[...], down_v[n * 256:(n + 1) * 256, :])
        y_out[n] = part[there, cols].astype(BF16)
        copy = pltpu.make_async_remote_copy(
            src_ref=y_out.at[n], dst_ref=y_in.at[n], send_sem=y_ssem.at[n], recv_sem=y_rsem.at[n],
            device_id=pair, device_id_type=MESH,
        )
        copy.start()
        y_copies.append(copy)
    for n in range(4):
        cols = pl.ds(n * 256, 256)
        y_copies[n].wait_recv()
        y_ref[:, cols] = (resid[here, cols] + part[here, cols] + y_in[n].astype(F32)).astype(BF16)

    first63 = pl.ds(0, n_seq - 1)
    pltpu.make_async_copy(lab_in.at[first63], lab_in.at[first63], a2a_sem.at[0]).wait()
    pltpu.make_async_copy(send.at[first63], send.at[first63], a2a_sem.at[2]).wait()
    for index_s in range(3):
        for k in range(chunks):
            sent(0, k, index_s)
    for copy in shipped:
        copy.wait_send()
    att_copy.wait_send()
    for copy in y_copies:
        copy.wait_send()


def shards(chunks, patch_tokens, keep_mask, slot_index, tile_map, qkv_proj, out_proj, up_proj, down_proj):
    n_seq = lax.axis_size("seq")
    freq = jnp.asarray((10000.0 ** (-np.arange(QUART) / QUART)).astype(np.float32)).reshape(1, QUART)
    qkv = jnp.transpose(qkv_proj, (1, 2, 0, 3)).reshape(3, D, HALF)
    hbm = pl.BlockSpec(memory_space=pl.ANY)
    vmem = pl.BlockSpec(memory_space=pltpu.VMEM)
    y = pl.pallas_call(
        functools.partial(kernel, n_seq, chunks),
        name="encoder_layer",
        out_shape=jax.ShapeDtypeStruct((64, D), BF16),
        in_specs=[pl.BlockSpec(memory_space=pltpu.SMEM), vmem, vmem, vmem, hbm, hbm, hbm, hbm, hbm],
        out_specs=vmem,
        scratch_shapes=[
            pltpu.VMEM((256, HALF), BF16),
            pltpu.VMEM((3, D, HALF), BF16),
            pltpu.VMEM((D, D), BF16),
            pltpu.VMEM((D, 2048), BF16),
            pltpu.VMEM((D, 2048), BF16),
            pltpu.VMEM((2, 256, QUART), BF16),
            pltpu.VMEM((n_seq, 8, QUART), BF16),
            pltpu.VMEM((n_seq, 8, QUART), BF16),
            pltpu.VMEM((1, 128), F32),
            pltpu.VMEM((n_seq, 1, 128), F32),
            pltpu.VMEM((2, 2, 128, HALF), BF16),
            pltpu.VMEM((128, D), BF16),
            pltpu.VMEM((128, HALF), BF16),
            pltpu.VMEM((256, HALF), BF16),
            pltpu.VMEM((256, HALF), BF16),
            pltpu.VMEM((2, 128, HALF), BF16),
            pltpu.VMEM((128, D), F32),
            pltpu.VMEM((128, D), BF16),
            pltpu.VMEM((128, 2048), BF16),
            pltpu.VMEM((128, D), F32),
            pltpu.VMEM((4, 64, 256), BF16),
            pltpu.VMEM((4, 64, 256), BF16),
            pltpu.SemaphoreType.DMA((5,)),
            pltpu.SemaphoreType.DMA((6,)),
            pltpu.SemaphoreType.DMA((3 * chunks,)),
            pltpu.SemaphoreType.DMA((3 * chunks,)),
            pltpu.SemaphoreType.DMA((14,)),
            pltpu.SemaphoreType.DMA((14,)),
            pltpu.SemaphoreType.DMA((2,)),
            pltpu.SemaphoreType.DMA((4,)),
            pltpu.SemaphoreType.DMA((4,)),
        ],
        compiler_params=pltpu.CompilerParams(
            collective_id=0, has_side_effects=True, vmem_limit_bytes=50 * 1024 * 1024
        ),
    )(tile_map, keep_mask, slot_index, freq, patch_tokens, qkv, out_proj, up_proj, down_proj)
    return y[None]


def solution(mesh):
    placed = (
        P("fsdp", "seq", None),
        P("fsdp", "seq"),
        P("fsdp", "seq"),
        P("fsdp", "seq"),
        P(None, "canvas", None, None),
        P(),
        P("fsdp", "canvas"),
        P("fsdp", "canvas"),
    )
    return jax.shard_map(
        functools.partial(shards, 2),
        mesh=mesh,
        in_specs=placed,
        out_specs=P("fsdp", ("seq", "canvas"), None),
        check_vma=False,
    )
```

```python
import functools

import jax
import jax.numpy as jnp
import numpy as np
from jax import lax
from jax.experimental import pallas as pl
from jax.experimental.pallas import tpu as pltpu
from jax.sharding import PartitionSpec as P

D = 1024
HALF = 512
QUART = 256
EPS = 1e-06
MESH = pl.DeviceIdType.MESH
F32 = jnp.float32
BF16 = jnp.bfloat16


def normalised(values):
    centered = values - jnp.mean(values, axis=-1, keepdims=True)
    spread = jnp.mean(centered * centered, axis=-1, keepdims=True)
    return centered * lax.rsqrt(spread + EPS)


def matmul(left, right):
    return jnp.dot(left, right, preferred_element_type=F32)


def matmul_nt(left, right):
    return lax.dot_general(left, right, (((1,), (1,)), ((), ())), preferred_element_type=F32)


def gelu(x):
    return 0.5 * x * (1.0 + lax.erf(x * (0.5**0.5)))


def kernel(
    n_seq, chunks,
    tile_hbm, keep_hbm, slot_hbm, freq_hbm, patch_hbm, qkv_hbm, out_hbm, up_hbm, down_hbm,
    y_ref,
    tile_ref, keep_ref, slot_ref, freq_ref, patch_v, qkv_v, out_v, up_v, down_v,
    emb, send, recv, lab_out, lab_in, vis, normed, q_s, k_s, v_s, att, resid, normed2, hidden, part, y_out, y_in,
    load_sem, a2a_sem, vis_ssem, vis_rsem, w_ssem, w_rsem, att_sem, y_ssem, y_rsem,
):
    s = lax.axis_index("seq")
    f = lax.axis_index("fsdp")
    c = lax.axis_index("canvas")
    other = 1 - c
    f_right, f_left, f_far = lax.rem(f + 2, 8), lax.rem(f + 6, 8), lax.rem(f + 4, 8)
    mate = f + 1 - 2 * lax.rem(f, 2)
    m_right, m_left, m_far = lax.rem(mate + 2, 8), lax.rem(mate + 6, 8), lax.rem(mate + 4, 8)
    s_next = lax.rem(s + 1, n_seq)
    s_diag = lax.rem(s + n_seq + 2 * c - 1, n_seq)

    barrier = pltpu.get_barrier_semaphore()

    def greet(i, carry):
        pl.semaphore_signal(barrier, inc=1, device_id={"seq": lax.rem(s + i, n_seq)}, device_id_type=MESH)
        return carry

    lax.fori_loop(1, n_seq, greet, 0)
    for peer in (f_right, f_left, mate):
        pl.semaphore_signal(barrier, inc=1, device_id={"fsdp": peer}, device_id_type=MESH)
    pl.semaphore_signal(barrier, inc=1, device_id={"canvas": other}, device_id_type=MESH)
    pl.semaphore_signal(barrier, inc=1, device_id={"seq": s_diag, "canvas": other}, device_id_type=MESH)

    col0 = pl.multiple_of(c * HALF, HALF)
    patch_load = pltpu.make_async_copy(patch_hbm.at[0, :, pl.ds(col0, HALF)], patch_v, load_sem.at[0])
    qkv_load = pltpu.make_async_copy(qkv_hbm, qkv_v, load_sem.at[1])
    out_load = pltpu.make_async_copy(out_hbm, out_v, load_sem.at[2])

    def rows_of(shard):
        return pl.ds(pl.multiple_of(shard * 128, 128), 128)

    up_load = pltpu.make_async_copy(up_hbm, up_v.at[rows_of(f)], load_sem.at[3])
    down_load = pltpu.make_async_copy(down_hbm, down_v.at[rows_of(f)], load_sem.at[4])
    index_loads = [
        pltpu.make_async_copy(keep_hbm, keep_ref, load_sem.at[5]),
        pltpu.make_async_copy(slot_hbm, slot_ref, load_sem.at[6]),
        pltpu.make_async_copy(freq_hbm, freq_ref, load_sem.at[7]),
        pltpu.make_async_copy(tile_hbm, tile_ref, load_sem.at[8]),
    ]
    for load in index_loads:
        load.start()
    for load in (patch_load, qkv_load, out_load, up_load, down_load):
        load.start()

    for load in index_loads:
        load.wait()
    slot = slot_ref[...]
    kept = keep_ref[...] == 1
    target = slot // 128
    lane4 = lax.rem(slot, 4)
    group = lax.rem(slot, 128) // 4
    first = jnp.where(kept & (lane4 == 0), target, -1)
    group_val = jnp.broadcast_to((group + 1).astype(F32), (8, 256)).astype(BF16)
    t_rows = lax.broadcasted_iota(jnp.int32, (128, 256), 0)
    hit = jnp.where(t_rows == first, 1.0, 0.0).astype(BF16)
    labels = matmul_nt(group_val, hit)
    lab_out[...] = labels[0:1, :]

    patch_load.wait()
    freq = freq_ref[...]
    within = lax.broadcasted_iota(jnp.int32, (16, QUART), 0)
    cell = jnp.where(c == 0, within // 4, lax.rem(within, 4))

    def embed(t, carry):
        tile = tile_ref[0, t]
        base = jnp.where(c == 0, tile // 32, lax.rem(tile, 32)) * 4
        angle = (base + cell).astype(F32) * freq
        rows = pl.ds(pl.multiple_of(t * 16, 16), 16)
        emb[0, rows, :] = (patch_v[rows, 0:QUART].astype(F32) + jnp.sin(angle)).astype(BF16)
        emb[1, rows, :] = (patch_v[rows, QUART:HALF].astype(F32) + jnp.cos(angle)).astype(BF16)
        return carry

    lax.fori_loop(0, 16, embed, 0)

    key = jnp.where(kept, target * 4 + lane4, -1000)
    row_i = lax.broadcasted_iota(jnp.int32, (512, QUART), 0)
    row_key = row_i // 8 * 4 + lax.rem(row_i, 4) + lax.rem(row_i // 4, 2) * 256
    pick0 = jnp.where(row_key == key, 1.0, 0.0).astype(BF16)
    pick1 = jnp.where(row_key == key + 256, 1.0, 0.0).astype(BF16)
    packed = matmul(pick0, emb[0]) + matmul(pick1, emb[1])
    send[...] = packed.astype(BF16).reshape(n_seq, 8, QUART)

    pl.semaphore_wait(barrier, n_seq + 4)

    def push(i, carry):
        step = 32 + (i + 1) // 2 * (2 * lax.rem(i, 2) - 1)
        to = lax.rem(s + step, n_seq)
        pltpu.make_async_remote_copy(
            src_ref=lab_out, dst_ref=lab_in.at[s], send_sem=a2a_sem.at[0], recv_sem=a2a_sem.at[1],
            device_id={"seq": to}, device_id_type=MESH,
        ).start()
        pltpu.make_async_remote_copy(
            src_ref=send.at[to], dst_ref=recv.at[s], send_sem=a2a_sem.at[2], recv_sem=a2a_sem.at[3],
            device_id={"seq": to}, device_id_type=MESH,
        ).start()
        return carry

    lax.fori_loop(0, n_seq - 1, push, 0)
    own_label = pltpu.make_async_copy(lab_out, lab_in.at[s], a2a_sem.at[4])
    own_label.start()
    own_rows = pltpu.make_async_copy(send.at[s], recv.at[s], a2a_sem.at[5])
    own_rows.start()

    def ship(src, buf, shard, to, index_s, index_r):
        copy = pltpu.make_async_remote_copy(
            src_ref=src, dst_ref=buf.at[rows_of(shard)], send_sem=w_ssem.at[index_s], recv_sem=w_rsem.at[index_r],
            device_id={"fsdp": to}, device_id_type=MESH,
        )
        copy.start()
        return copy

    def landed(buf, shard, index_r):
        view = buf.at[rows_of(shard)]
        pltpu.make_async_copy(view, view, w_rsem.at[index_r]).wait()

    shipped = [
        ship(up_hbm, up_v, f, f_right, 0, 0),
        ship(down_hbm, down_v, f, f_left, 1, 3),
        ship(down_hbm, down_v, f, f_right, 2, 1),
        ship(up_hbm, up_v, f, f_left, 3, 2),
        ship(up_hbm, up_v, f, mate, 4, 6),
        ship(down_hbm, down_v, f, mate, 5, 7),
    ]

    own_label.wait()
    pltpu.make_async_copy(lab_in.at[pl.ds(0, n_seq - 1)], lab_in.at[pl.ds(0, n_seq - 1)], a2a_sem.at[1]).wait()
    lane_of = lax.broadcasted_iota(jnp.int32, (8, 128), 1)
    mine = jnp.where(lane_of == s, 1.0, 0.0).astype(BF16)
    came = matmul_nt(mine, lab_in[...].reshape(n_seq, 128).astype(BF16))
    spread_r = lax.broadcasted_iota(jnp.int32, (n_seq, 512), 0)
    spread_c = lax.broadcasted_iota(jnp.int32, (n_seq, 512), 1)
    spread = jnp.where(spread_r == spread_c // 8, 1.0, 0.0).astype(BF16)
    label_of = matmul(came.astype(BF16), spread).astype(jnp.int32)
    col_i = lax.broadcasted_iota(jnp.int32, (8, 512), 1)
    row_of = label_of * 4 - 4 + lax.rem(col_i, 4)
    half_of = lax.rem(col_i // 4, 2)
    r_i = lax.broadcasted_iota(jnp.int32, (128, 512), 0)
    places = []
    for h in range(2):
        row_h = jnp.where(half_of == h, row_of, -1)[0:1, :]
        places.append(jnp.where(r_i == row_h, 1.0, 0.0).astype(BF16))
    own_rows.wait()
    pltpu.make_async_copy(recv.at[pl.ds(0, n_seq - 1)], recv.at[pl.ds(0, n_seq - 1)], a2a_sem.at[3]).wait()
    came_rows = recv[...].reshape(512, QUART)
    for h in range(2):
        vis[0, c, :, h * QUART:(h + 1) * QUART] = matmul(places[h], came_rows).astype(BF16)

    size = 128 // chunks

    def view_of(block, half, k):
        return vis.at[block, half, pl.ds(k * size, size), :]

    def pass_on(half, src_block, dst_block, k, to, index_s, index_r):
        copy = pltpu.make_async_remote_copy(
            src_ref=view_of(src_block, half, k), dst_ref=view_of(dst_block, half, k),
            send_sem=vis_ssem.at[index_s * chunks + k], recv_sem=vis_rsem.at[index_r * chunks + k],
            device_id=to, device_id_type=MESH,
        )
        copy.start()
        return copy

    def arrived(block, half, k, index_r):
        view = view_of(block, half, k)
        pltpu.make_async_copy(view, view, vis_rsem.at[index_r * chunks + k]).wait()

    def sent(half, k, index_s):
        view = view_of(0, half, k)
        pltpu.make_async_copy(view, view, vis_ssem.at[index_s * chunks + k]).wait()

    pair = {"canvas": other}
    onward = {"seq": s_next, "canvas": 0}
    for k in range(chunks):
        pass_on(c, 0, 0, k, pair, 0, 0)

    @pl.when(c == 1)
    def _():
        for k in range(chunks):
            pass_on(1, 0, 1, k, onward, 1, 1)
        for k in range(chunks):
            arrived(0, 0, k, 0)
            pass_on(0, 0, 1, k, onward, 2, 2)

    @pl.when(c == 0)
    def _():
        for k in range(chunks):
            arrived(1, 1, k, 1)
            pass_on(1, 1, 1, k, pair, 1, 1)
        for k in range(chunks):
            arrived(0, 1, k, 0)

    landed(up_v, f_left, 0)
    shipped.append(ship(up_v.at[rows_of(f_left)], up_v, f_left, f_right, 6, 4))
    landed(down_v, f_right, 3)
    shipped.append(ship(down_v.at[rows_of(f_right)], down_v, f_right, f_left, 7, 5))
    shipped.append(ship(up_v.at[rows_of(f_left)], up_v, f_left, mate, 8, 8))
    shipped.append(ship(down_v.at[rows_of(f_right)], down_v, f_right, mate, 9, 11))

    qkv_load.wait()
    visible = jnp.concatenate([vis[0, 0], vis[0, 1]], axis=1).astype(F32)
    normed[...] = normalised(visible).astype(BF16)
    q_s[...] = matmul(normed[...], qkv_v[0]).astype(BF16)
    k_s[0:128, :] = matmul(normed[...], qkv_v[1]).astype(BF16)
    v_s[0:128, :] = matmul(normed[...], qkv_v[2]).astype(BF16)

    @pl.when(c == 0)
    def _():
        for k in range(chunks):
            arrived(1, 0, k, 2)
            pass_on(0, 1, 1, k, pair, 2, 2)

    @pl.when(c == 1)
    def _():
        for k in range(chunks):
            arrived(1, 1, k, 1)
        for k in range(chunks):
            arrived(1, 0, k, 2)

    before = jnp.concatenate([vis[1, 0], vis[1, 1]], axis=1).astype(F32)
    normed[...] = normalised(before).astype(BF16)
    k_s[128:256, :] = matmul(normed[...], qkv_v[1]).astype(BF16)
    v_s[128:256, :] = matmul(normed[...], qkv_v[2]).astype(BF16)

    low = lax.broadcasted_iota(jnp.int32, (128, 128), 1) < 64
    for p in range(4):
        lanes = pl.ds(p * 128, 128)
        q_pair, k_pair, v_pair = q_s[:, lanes], k_s[:, lanes], v_s[:, lanes]
        mixed = []
        for e in range(2):
            q_one = jnp.where(low == (e == 0), q_pair.astype(F32), 0.0).astype(BF16)
            scores = matmul_nt(q_one, k_pair) * 0.125
            expo = jnp.exp(scores - jnp.max(scores, axis=-1, keepdims=True))
            total = jnp.sum(expo, axis=-1, keepdims=True)
            mixed.append(matmul(expo.astype(BF16), v_pair) / total)
        att[c, :, lanes] = jnp.where(low, mixed[0], mixed[1]).astype(BF16)

    att_copy = pltpu.make_async_remote_copy(
        src_ref=att.at[c], dst_ref=att.at[c], send_sem=att_sem.at[0], recv_sem=att_sem.at[1],
        device_id=pair, device_id_type=MESH,
    )
    att_copy.start()

    landed(down_v, f_left, 1)
    shipped.append(ship(down_v.at[rows_of(f_left)], down_v, f_left, mate, 10, 9))
    landed(up_v, f_right, 2)
    shipped.append(ship(up_v.at[rows_of(f_right)], up_v, f_right, mate, 11, 10))

    out_load.wait()
    att_copy.wait_recv()
    mixed_in = jnp.concatenate([att[0], att[1]], axis=1)
    visible = jnp.concatenate([vis[0, 0], vis[0, 1]], axis=1).astype(F32)
    resid[...] = visible + matmul(mixed_in, out_v[...])
    normed2[...] = normalised(resid[...]).astype(BF16)

    landed(up_v, f_far, 4)
    shipped.append(ship(up_v.at[rows_of(f_far)], up_v, f_far, mate, 12, 12))
    landed(down_v, f_far, 5)
    shipped.append(ship(down_v.at[rows_of(f_far)], down_v, f_far, mate, 13, 13))

    up_load.wait()
    down_load.wait()
    landed(up_v, mate, 6)
    landed(up_v, m_left, 8)
    landed(up_v, m_right, 10)
    landed(up_v, m_far, 12)

    def widen(n, carry):
        cols = pl.ds(pl.multiple_of(n * 256, 256), 256)
        hidden[:, cols] = gelu(matmul(normed2[...], up_v[:, cols])).astype(BF16)
        return carry

    lax.fori_loop(0, 8, widen, 0)

    landed(down_v, mate, 7)
    landed(down_v, m_left, 9)
    landed(down_v, m_right, 11)
    landed(down_v, m_far, 13)

    here = pl.ds(pl.multiple_of(c * 64, 64), 64)
    there = pl.ds(pl.multiple_of(other * 64, 64), 64)
    y_copies = []
    for n in range(4):
        cols = pl.ds(n * 256, 256)
        part[:, cols] = matmul_nt(hidden[...], down_v[n * 256:(n + 1) * 256, :])
        y_out[n] = part[there, cols].astype(BF16)
        copy = pltpu.make_async_remote_copy(
            src_ref=y_out.at[n], dst_ref=y_in.at[n], send_sem=y_ssem.at[n], recv_sem=y_rsem.at[n],
            device_id=pair, device_id_type=MESH,
        )
        copy.start()
        y_copies.append(copy)
    for n in range(4):
        cols = pl.ds(n * 256, 256)
        y_copies[n].wait_recv()
        y_ref[:, cols] = (resid[here, cols] + part[here, cols] + y_in[n].astype(F32)).astype(BF16)

    first63 = pl.ds(0, n_seq - 1)
    pltpu.make_async_copy(lab_in.at[first63], lab_in.at[first63], a2a_sem.at[0]).wait()
    pltpu.make_async_copy(send.at[first63], send.at[first63], a2a_sem.at[2]).wait()
    for index_s in range(3):
        for k in range(chunks):
            sent(0, k, index_s)
    for copy in shipped:
        copy.wait_send()
    att_copy.wait_send()
    for copy in y_copies:
        copy.wait_send()


def shards(chunks, patch_tokens, keep_mask, slot_index, tile_map, qkv_proj, out_proj, up_proj, down_proj):
    n_seq = lax.axis_size("seq")
    freq = jnp.asarray((10000.0 ** (-np.arange(QUART) / QUART)).astype(np.float32)).reshape(1, QUART)
    qkv = jnp.transpose(qkv_proj, (1, 2, 0, 3)).reshape(3, D, HALF)
    hbm = pl.BlockSpec(memory_space=pltpu.HBM)
    vmem = pl.BlockSpec(memory_space=pltpu.VMEM)
    y = pl.pallas_call(
        functools.partial(kernel, n_seq, chunks),
        name="encoder_layer",
        out_shape=jax.ShapeDtypeStruct((64, D), BF16),
        in_specs=[hbm] * 9,
        out_specs=vmem,
        scratch_shapes=[
            pltpu.SMEM((1, 16), jnp.int32),
            pltpu.VMEM((1, 256), jnp.int32),
            pltpu.VMEM((1, 256), jnp.int32),
            pltpu.VMEM((1, QUART), F32),
            pltpu.VMEM((256, HALF), BF16),
            pltpu.VMEM((3, D, HALF), BF16),
            pltpu.VMEM((D, D), BF16),
            pltpu.VMEM((D, 2048), BF16),
            pltpu.VMEM((D, 2048), BF16),
            pltpu.VMEM((2, 256, QUART), BF16),
            pltpu.VMEM((n_seq, 8, QUART), BF16),
            pltpu.VMEM((n_seq, 8, QUART), BF16),
            pltpu.VMEM((1, 128), F32),
            pltpu.VMEM((n_seq, 1, 128), F32),
            pltpu.VMEM((2, 2, 128, HALF), BF16),
            pltpu.VMEM((128, D), BF16),
            pltpu.VMEM((128, HALF), BF16),
            pltpu.VMEM((256, HALF), BF16),
            pltpu.VMEM((256, HALF), BF16),
            pltpu.VMEM((2, 128, HALF), BF16),
            pltpu.VMEM((128, D), F32),
            pltpu.VMEM((128, D), BF16),
            pltpu.VMEM((128, 2048), BF16),
            pltpu.VMEM((128, D), F32),
            pltpu.VMEM((4, 64, 256), BF16),
            pltpu.VMEM((4, 64, 256), BF16),
            pltpu.SemaphoreType.DMA((9,)),
            pltpu.SemaphoreType.DMA((6,)),
            pltpu.SemaphoreType.DMA((3 * chunks,)),
            pltpu.SemaphoreType.DMA((3 * chunks,)),
            pltpu.SemaphoreType.DMA((14,)),
            pltpu.SemaphoreType.DMA((14,)),
            pltpu.SemaphoreType.DMA((2,)),
            pltpu.SemaphoreType.DMA((4,)),
            pltpu.SemaphoreType.DMA((4,)),
        ],
        compiler_params=pltpu.CompilerParams(
            collective_id=0, has_side_effects=True, vmem_limit_bytes=67043328
        ),
    )(tile_map, keep_mask, slot_index, freq, patch_tokens, qkv, out_proj, up_proj, down_proj)
    return y[None]


def solution(mesh):
    placed = (
        P("fsdp", "seq", None),
        P("fsdp", "seq"),
        P("fsdp", "seq"),
        P("fsdp", "seq"),
        P(None, "canvas", None, None),
        P(),
        P("fsdp", "canvas"),
        P("fsdp", "canvas"),
    )
    return jax.shard_map(
        functools.partial(shards, 2),
        mesh=mesh,
        in_specs=placed,
        out_specs=P("fsdp", ("seq", "canvas"), None),
        check_vma=False,
    )
```

```python
import functools

import jax
import jax.numpy as jnp
import numpy as np
from jax import lax
from jax.experimental import pallas as pl
from jax.experimental.pallas import tpu as pltpu
from jax.sharding import PartitionSpec as P

D = 1024
HALF = 512
QUART = 256
EPS = 1e-06
MESH = pl.DeviceIdType.MESH
F32 = jnp.float32
BF16 = jnp.bfloat16


def normalised(values):
    centered = values - jnp.mean(values, axis=-1, keepdims=True)
    spread = jnp.mean(centered * centered, axis=-1, keepdims=True)
    return centered * lax.rsqrt(spread + EPS)


def matmul(left, right):
    return jnp.dot(left, right, preferred_element_type=F32)


def matmul_nt(left, right):
    return lax.dot_general(left, right, (((1,), (1,)), ((), ())), preferred_element_type=F32)


def gelu(x):
    return 0.5 * x * (1.0 + lax.erf(x * (0.5**0.5)))


def kernel(
    n_seq, chunks,
    tile_hbm, keep_hbm, slot_hbm, freq_hbm, patch_hbm, qkv_hbm, out_hbm, up_hbm, down_hbm,
    y_ref,
    tile_ref, keep_ref, slot_ref, freq_ref, patch_v, qkv_v, out_v, up_v, down_v,
    emb, send, recv, lab_out, lab_in, vis, normed, q_s, k_s, v_s, att, resid, normed2, hidden, part, y_out, y_in,
    load_sem, a2a_sem, vis_ssem, vis_rsem, w_ssem, w_rsem, att_sem, y_ssem, y_rsem,
):
    s = lax.axis_index("seq")
    f = lax.axis_index("fsdp")
    c = lax.axis_index("canvas")
    other = 1 - c
    f_right, f_left, f_far = lax.rem(f + 2, 8), lax.rem(f + 6, 8), lax.rem(f + 4, 8)
    mate = f + 1 - 2 * lax.rem(f, 2)
    m_right, m_left, m_far = lax.rem(mate + 2, 8), lax.rem(mate + 6, 8), lax.rem(mate + 4, 8)
    block_in = lax.rem(s + n_seq - c, n_seq)
    s_diag = lax.rem(s + n_seq + 2 * c - 1, n_seq)

    barrier = pltpu.get_barrier_semaphore()

    def far_first(i):
        return n_seq // 2 + (i + 1) // 2 * (2 * lax.rem(i, 2) - 1)

    def greet(i, carry):
        peer = lax.rem(s + far_first(i), n_seq)
        pl.semaphore_signal(barrier, inc=1, device_id={"seq": peer}, device_id_type=MESH)
        return carry

    lax.fori_loop(0, n_seq - 1, greet, 0)
    for peer in (f_right, f_left, mate):
        pl.semaphore_signal(barrier, inc=1, device_id={"fsdp": peer}, device_id_type=MESH)
    pl.semaphore_signal(barrier, inc=1, device_id={"canvas": other}, device_id_type=MESH)
    pl.semaphore_signal(barrier, inc=1, device_id={"seq": s_diag, "canvas": other}, device_id_type=MESH)

    col0 = pl.multiple_of(c * HALF, HALF)
    patch_load = pltpu.make_async_copy(patch_hbm.at[0, :, pl.ds(col0, HALF)], patch_v, load_sem.at[0])
    qkv_load = pltpu.make_async_copy(qkv_hbm, qkv_v, load_sem.at[1])
    out_load = pltpu.make_async_copy(out_hbm, out_v, load_sem.at[2])

    def rows_of(shard):
        return pl.ds(pl.multiple_of(shard * 128, 128), 128)

    up_load = pltpu.make_async_copy(up_hbm, up_v.at[rows_of(f)], load_sem.at[3])
    down_load = pltpu.make_async_copy(down_hbm, down_v.at[rows_of(f)], load_sem.at[4])
    index_loads = [
        pltpu.make_async_copy(keep_hbm, keep_ref, load_sem.at[5]),
        pltpu.make_async_copy(slot_hbm, slot_ref, load_sem.at[6]),
        pltpu.make_async_copy(freq_hbm, freq_ref, load_sem.at[7]),
        pltpu.make_async_copy(tile_hbm, tile_ref, load_sem.at[8]),
    ]
    for load in index_loads:
        load.start()
    for load in (patch_load, qkv_load, out_load, up_load, down_load):
        load.start()

    for load in index_loads:
        load.wait()
    slot = slot_ref[...]
    kept = keep_ref[...] == 1
    target = slot // 128
    lane4 = lax.rem(slot, 4)
    group = lax.rem(slot, 128) // 4
    first = jnp.where(kept & (lane4 == 0), target, -1)
    group_val = jnp.broadcast_to((group + 1).astype(F32), (8, 256)).astype(BF16)
    t_rows = lax.broadcasted_iota(jnp.int32, (128, 256), 0)
    hit = jnp.where(t_rows == first, 1.0, 0.0).astype(BF16)
    labels = matmul_nt(group_val, hit)
    lab_out[...] = labels[0:1, :]

    patch_load.wait()
    freq = freq_ref[...]
    within = lax.broadcasted_iota(jnp.int32, (16, QUART), 0)
    cell = jnp.where(c == 0, within // 4, lax.rem(within, 4))

    def embed(t, carry):
        tile = tile_ref[0, t]
        base = jnp.where(c == 0, tile // 32, lax.rem(tile, 32)) * 4
        angle = (base + cell).astype(F32) * freq
        rows = pl.ds(pl.multiple_of(t * 16, 16), 16)
        emb[0, rows, :] = (patch_v[rows, 0:QUART].astype(F32) + jnp.sin(angle)).astype(BF16)
        emb[1, rows, :] = (patch_v[rows, QUART:HALF].astype(F32) + jnp.cos(angle)).astype(BF16)
        return carry

    lax.fori_loop(0, 16, embed, 0)

    key = jnp.where(kept, target * 4 + lane4, -1000)
    row_i = lax.broadcasted_iota(jnp.int32, (512, QUART), 0)
    row_key = row_i // 8 * 4 + lax.rem(row_i, 4) + lax.rem(row_i // 4, 2) * 256
    pick0 = jnp.where(row_key == key, 1.0, 0.0).astype(BF16)
    pick1 = jnp.where(row_key == key + 256, 1.0, 0.0).astype(BF16)
    packed = matmul(pick0, emb[0]) + matmul(pick1, emb[1])
    send[...] = packed.astype(BF16).reshape(n_seq, 8, QUART)

    pl.semaphore_wait(barrier, n_seq + 4)

    def push(i, carry):
        to = lax.rem(s + far_first(i), n_seq)
        block = lax.rem(to + n_seq - c, n_seq)
        pltpu.make_async_remote_copy(
            src_ref=lab_out, dst_ref=lab_in.at[s], send_sem=a2a_sem.at[0], recv_sem=a2a_sem.at[1],
            device_id={"seq": to}, device_id_type=MESH,
        ).start()
        pltpu.make_async_remote_copy(
            src_ref=send.at[block], dst_ref=recv.at[s], send_sem=a2a_sem.at[2], recv_sem=a2a_sem.at[3],
            device_id={"seq": to}, device_id_type=MESH,
        ).start()
        return carry

    lax.fori_loop(0, n_seq - 1, push, 0)
    own_label = pltpu.make_async_copy(lab_out, lab_in.at[s], a2a_sem.at[4])
    own_label.start()
    own_rows = pltpu.make_async_copy(send.at[block_in], recv.at[s], a2a_sem.at[5])
    own_rows.start()

    def piece(buf, shard, part):
        first_row, count = ((0, 64), (64, 64), (0, 128))[part]
        return buf.at[pl.ds(pl.multiple_of(shard * 128 + first_row, 64), count)]

    shipped = []

    def ship(buf, shard, part, to, index_r):
        copy = pltpu.make_async_remote_copy(
            src_ref=piece(buf, shard, part), dst_ref=piece(buf, shard, part),
            send_sem=w_ssem.at[len(shipped)], recv_sem=w_rsem.at[index_r],
            device_id={"fsdp": to}, device_id_type=MESH,
        )
        copy.start()
        shipped.append(copy)

    def landed(buf, shard, part, index_r):
        view = piece(buf, shard, part)
        pltpu.make_async_copy(view, view, w_rsem.at[index_r]).wait()

    up_load.wait()
    ship(up_v, f, 2, f_right, 0)
    ship(up_v, f, 2, f_left, 1)
    ship(up_v, f, 2, mate, 10)
    down_load.wait()
    ship(down_v, f, 0, f_right, 2)
    ship(down_v, f, 1, f_left, 5)
    ship(down_v, f, 2, mate, 11)

    own_label.wait()
    pltpu.make_async_copy(lab_in.at[pl.ds(0, n_seq - 1)], lab_in.at[pl.ds(0, n_seq - 1)], a2a_sem.at[1]).wait()
    lane_of = lax.broadcasted_iota(jnp.int32, (8, 128), 1)
    mine = jnp.where(lane_of == block_in, 1.0, 0.0).astype(BF16)
    came = matmul_nt(mine, lab_in[...].reshape(n_seq, 128).astype(BF16))
    spread_r = lax.broadcasted_iota(jnp.int32, (n_seq, 512), 0)
    spread_c = lax.broadcasted_iota(jnp.int32, (n_seq, 512), 1)
    spread = jnp.where(spread_r == spread_c // 8, 1.0, 0.0).astype(BF16)
    label_of = matmul(came.astype(BF16), spread).astype(jnp.int32)
    col_i = lax.broadcasted_iota(jnp.int32, (8, 512), 1)
    row_of = label_of * 4 - 4 + lax.rem(col_i, 4)
    half_of = lax.rem(col_i // 4, 2)
    r_i = lax.broadcasted_iota(jnp.int32, (128, 512), 0)
    places = []
    for h in range(2):
        row_h = jnp.where(half_of == h, row_of, -1)[0:1, :]
        places.append(jnp.where(r_i == row_h, 1.0, 0.0).astype(BF16))
    landed(up_v, f_left, 2, 0)
    ship(up_v, f_left, 0, f_right, 6)
    landed(up_v, f_right, 2, 1)
    ship(up_v, f_right, 1, f_left, 7)
    ship(down_v, f, 1, f_right, 3)
    ship(down_v, f, 0, f_left, 4)

    own_rows.wait()
    pltpu.make_async_copy(recv.at[pl.ds(0, n_seq - 1)], recv.at[pl.ds(0, n_seq - 1)], a2a_sem.at[3]).wait()
    came_rows = recv[...].reshape(512, QUART)
    size = 128 // chunks

    def view_of(block, half, k):
        return vis.at[block, half, pl.ds(k * size, size), :]

    def pass_on(block, half, to_block, k, to, leg):
        pltpu.make_async_remote_copy(
            src_ref=view_of(block, half, k), dst_ref=view_of(to_block, half, k),
            send_sem=vis_ssem.at[leg * chunks + k], recv_sem=vis_rsem.at[leg * chunks + k],
            device_id=to, device_id_type=MESH,
        ).start()

    def arrived(block, half, k, leg):
        view = view_of(block, half, k)
        pltpu.make_async_copy(view, view, vis_rsem.at[leg * chunks + k]).wait()

    def sent(k, leg):
        view = view_of(0, 0, k)
        pltpu.make_async_copy(view, view, vis_ssem.at[leg * chunks + k]).wait()

    pair = {"canvas": other}
    diagonal = {"seq": s_diag, "canvas": other}
    for k in range(chunks):
        for h in range(2):
            place = places[h][k * size:(k + 1) * size, :]
            vis[c, c, k * size:(k + 1) * size, h * QUART:(h + 1) * QUART] = matmul(place, came_rows).astype(BF16)
        pass_on(c, c, c, k, pair, 0)
    ship(up_v, f_left, 2, mate, 12)
    ship(up_v, f_right, 2, mate, 13)
    for k in range(chunks):
        arrived(other, other, k, 0)
        pass_on(other, other, c, k, diagonal, 1)
    for k in range(chunks):
        arrived(other, c, k, 1)
        pass_on(other, c, other, k, pair, 2)

    qkv_load.wait()

    def project(block):
        rows = pl.ds(pl.multiple_of(block * 128, 128), 128)
        normed[...] = normalised(jnp.concatenate([vis[block, 0], vis[block, 1]], axis=1).astype(F32)).astype(BF16)
        k_s[rows, :] = matmul(normed[...], qkv_v[1]).astype(BF16)
        v_s[rows, :] = matmul(normed[...], qkv_v[2]).astype(BF16)

        @pl.when(block == 0)
        def _():
            q_s[...] = matmul(normed[...], qkv_v[0]).astype(BF16)

    project(other)
    landed(up_v, f_far, 0, 6)
    landed(up_v, f_far, 1, 7)
    ship(up_v, f_far, 2, mate, 16)
    landed(down_v, f_left, 0, 2)
    ship(down_v, f_left, 0, f_right, 8)
    landed(down_v, f_right, 1, 5)
    ship(down_v, f_right, 1, f_left, 9)
    for k in range(chunks):
        arrived(c, other, k, 2)
    project(c)

    low = lax.broadcasted_iota(jnp.int32, (128, 128), 1) < 64
    att_copies = []
    for p in range(4):
        lanes = pl.ds(p * 128, 128)
        q_pair, k_pair, v_pair = q_s[:, lanes], k_s[:, lanes], v_s[:, lanes]
        mixed = []
        for e in range(2):
            q_one = jnp.where(low == (e == 0), q_pair.astype(F32), 0.0).astype(BF16)
            scores = matmul_nt(q_one, k_pair) * 0.125
            expo = jnp.exp(scores - jnp.max(scores, axis=-1, keepdims=True))
            total = jnp.sum(expo, axis=-1, keepdims=True)
            mixed.append(matmul(expo.astype(BF16), v_pair) / total)
        att[c, p] = jnp.where(low, mixed[0], mixed[1]).astype(BF16)
        copy = pltpu.make_async_remote_copy(
            src_ref=att.at[c, p], dst_ref=att.at[c, p], send_sem=att_sem.at[p], recv_sem=att_sem.at[4 + p],
            device_id=pair, device_id_type=MESH,
        )
        copy.start()
        att_copies.append(copy)

    landed(down_v, f_left, 1, 3)
    ship(down_v, f_left, 2, mate, 14)
    landed(down_v, f_right, 0, 4)
    ship(down_v, f_right, 2, mate, 15)

    out_load.wait()

    def mix(half):
        rows = pl.ds(pl.multiple_of(half * HALF, HALF), HALF)
        heads = jnp.concatenate([att[half, p] for p in range(4)], axis=1)
        return matmul(heads, out_v[rows, :])

    visible = jnp.concatenate([vis[0, 0], vis[0, 1]], axis=1).astype(F32)
    resid[...] = visible + mix(c)
    for copy in att_copies:
        copy.wait_recv()
    resid[...] += mix(other)
    normed2[...] = normalised(resid[...]).astype(BF16)

    landed(up_v, mate, 2, 10)
    landed(up_v, m_left, 2, 12)
    landed(up_v, m_right, 2, 13)
    landed(up_v, m_far, 2, 16)

    def widen(n, carry):
        cols = pl.ds(pl.multiple_of(n * 256, 256), 256)
        hidden[:, cols] = gelu(matmul(normed2[...], up_v[:, cols])).astype(BF16)
        return carry

    lax.fori_loop(0, 8, widen, 0)

    landed(down_v, f_far, 0, 8)
    landed(down_v, f_far, 1, 9)
    ship(down_v, f_far, 2, mate, 17)

    here = pl.ds(pl.multiple_of(c * 64, 64), 64)
    there = pl.ds(pl.multiple_of(other * 64, 64), 64)
    chip = f // 2
    y_copies = []
    for n, (step, shard, index_r) in enumerate(((0, mate, 11), (3, m_left, 14), (1, m_right, 15), (2, m_far, 17))):
        landed(down_v, shard, 2, index_r)
        cols = pl.ds(pl.multiple_of(lax.rem(chip + step, 4) * 256, 256), 256)
        part[:, cols] = matmul_nt(hidden[...], down_v[cols, :])
        y_out[n] = part[there, cols].astype(BF16)
        copy = pltpu.make_async_remote_copy(
            src_ref=y_out.at[n], dst_ref=y_in.at[n], send_sem=y_ssem.at[n], recv_sem=y_rsem.at[n],
            device_id=pair, device_id_type=MESH,
        )
        copy.start()
        y_copies.append(copy)
    for n, step in enumerate((0, 3, 1, 2)):
        cols = pl.ds(pl.multiple_of(lax.rem(chip + step, 4) * 256, 256), 256)
        y_copies[n].wait_recv()
        y_ref[:, cols] = (resid[here, cols] + part[here, cols] + y_in[n].astype(F32)).astype(BF16)

    first63 = pl.ds(0, n_seq - 1)
    pltpu.make_async_copy(lab_in.at[first63], lab_in.at[first63], a2a_sem.at[0]).wait()
    pltpu.make_async_copy(send.at[first63], send.at[first63], a2a_sem.at[2]).wait()
    for leg in range(3):
        for k in range(chunks):
            sent(k, leg)
    for copy in shipped:
        copy.wait_send()
    for copy in att_copies + y_copies:
        copy.wait_send()


def shards(chunks, patch_tokens, keep_mask, slot_index, tile_map, qkv_proj, out_proj, up_proj, down_proj):
    n_seq = lax.axis_size("seq")
    freq = jnp.asarray((10000.0 ** (-np.arange(QUART) / QUART)).astype(np.float32)).reshape(1, QUART)
    qkv = jnp.transpose(qkv_proj, (1, 2, 0, 3)).reshape(3, D, HALF)
    hbm = pl.BlockSpec(memory_space=pltpu.HBM)
    vmem = pl.BlockSpec(memory_space=pltpu.VMEM)
    y = pl.pallas_call(
        functools.partial(kernel, n_seq, chunks),
        name="encoder_layer",
        out_shape=pltpu.VMEM((64, D), BF16),
        in_specs=[hbm] * 9,
        out_specs=vmem,
        scratch_shapes=[
            pltpu.SMEM((1, 16), jnp.int32),
            pltpu.VMEM((1, 256), jnp.int32),
            pltpu.VMEM((1, 256), jnp.int32),
            pltpu.VMEM((1, QUART), F32),
            pltpu.VMEM((256, HALF), BF16),
            pltpu.VMEM((3, D, HALF), BF16),
            pltpu.VMEM((D, D), BF16),
            pltpu.VMEM((D, 2048), BF16),
            pltpu.VMEM((D, 2048), BF16),
            pltpu.VMEM((2, 256, QUART), BF16),
            pltpu.VMEM((n_seq, 8, QUART), BF16),
            pltpu.VMEM((n_seq, 8, QUART), BF16),
            pltpu.VMEM((1, 128), F32),
            pltpu.VMEM((n_seq, 1, 128), F32),
            pltpu.VMEM((2, 2, 128, HALF), BF16),
            pltpu.VMEM((128, D), BF16),
            pltpu.VMEM((128, HALF), BF16),
            pltpu.VMEM((256, HALF), BF16),
            pltpu.VMEM((256, HALF), BF16),
            pltpu.VMEM((2, 4, 128, 128), BF16),
            pltpu.VMEM((128, D), F32),
            pltpu.VMEM((128, D), BF16),
            pltpu.VMEM((128, 2048), BF16),
            pltpu.VMEM((128, D), F32),
            pltpu.VMEM((4, 64, 256), BF16),
            pltpu.VMEM((4, 64, 256), BF16),
            pltpu.SemaphoreType.DMA((9,)),
            pltpu.SemaphoreType.DMA((6,)),
            pltpu.SemaphoreType.DMA((3 * chunks,)),
            pltpu.SemaphoreType.DMA((3 * chunks,)),
            pltpu.SemaphoreType.DMA((18,)),
            pltpu.SemaphoreType.DMA((18,)),
            pltpu.SemaphoreType.DMA((8,)),
            pltpu.SemaphoreType.DMA((4,)),
            pltpu.SemaphoreType.DMA((4,)),
        ],
        compiler_params=pltpu.CompilerParams(
            collective_id=0, has_side_effects=True, vmem_limit_bytes=58 * 1024 * 1024
        ),
    )(*[
        pltpu.with_memory_space_constraint(operand, pltpu.HBM)
        for operand in (tile_map, keep_mask, slot_index, freq, patch_tokens, qkv, out_proj, up_proj, down_proj)
    ])
    return y[None]


def solution(mesh):
    placed = (
        P("fsdp", "seq", None),
        P("fsdp", "seq"),
        P("fsdp", "seq"),
        P("fsdp", "seq"),
        P(None, "canvas", None, None),
        P(),
        P("fsdp", "canvas"),
        P("fsdp", "canvas"),
    )
    return jax.shard_map(
        functools.partial(shards, 4),
        mesh=mesh,
        in_specs=placed,
        out_specs=P("fsdp", ("seq", "canvas"), None),
        check_vma=False,
    )
```

```python
import functools

import jax
import jax.numpy as jnp
import numpy as np
from jax import lax
from jax.experimental import pallas as pl
from jax.experimental.pallas import tpu as pltpu
from jax.sharding import PartitionSpec as P

D = 1024
HALF = 512
QUART = 256
EPS = 1e-06
MESH = pl.DeviceIdType.MESH
F32 = jnp.float32
BF16 = jnp.bfloat16


def normalised(values):
    centered = values - jnp.mean(values, axis=-1, keepdims=True)
    spread = jnp.mean(centered * centered, axis=-1, keepdims=True)
    return centered * lax.rsqrt(spread + EPS)


def matmul(left, right):
    return jnp.dot(left, right, preferred_element_type=F32)


def matmul_nt(left, right):
    return lax.dot_general(left, right, (((1,), (1,)), ((), ())), preferred_element_type=F32)


def gelu(x):
    return 0.5 * x * (1.0 + lax.erf(x * (0.5**0.5)))


def kernel(
    n_seq, chunks,
    tile_hbm, keep_hbm, slot_hbm, freq_hbm, patch_hbm, qkv_hbm, out_hbm, up_hbm, down_hbm,
    y_ref,
    tile_ref, keep_ref, slot_ref, freq_ref, patch_v, qkv_v, out_v, up_v, down_v,
    emb, send, recv, lab_out, lab_in, vis, normed, q_s, k_s, v_s, att, resid, normed2, hidden, part, y_out, y_in,
    met_sem, load_sem, a2a_sem, vis_ssem, vis_rsem, w_ssem, w_rsem, att_sem, y_ssem, y_rsem,
):
    s = lax.axis_index("seq")
    f = lax.axis_index("fsdp")
    c = lax.axis_index("canvas")
    other = 1 - c
    f_right, f_left, f_far = lax.rem(f + 2, 8), lax.rem(f + 6, 8), lax.rem(f + 4, 8)
    mate = f + 1 - 2 * lax.rem(f, 2)
    m_right, m_left, m_far = lax.rem(mate + 2, 8), lax.rem(mate + 6, 8), lax.rem(mate + 4, 8)
    block_in = lax.rem(s + n_seq - c, n_seq)
    s_diag = lax.rem(s + n_seq + 2 * c - 1, n_seq)

    barrier = pltpu.get_barrier_semaphore()
    n_z = n_seq // 4
    z, y_hi = s // 4, lax.rem(s, 4)
    n_near, n_far = n_seq // 2 + 3, n_seq // 2 - 4

    def peer_at(dz, dy):
        return lax.rem(z + dz + n_z, n_z) * 4 + lax.rem(y_hi + dy, 4)

    def near_peer(j):
        i = j // 4
        return peer_at((n_z // 4 - i // 2) * (1 - 2 * lax.rem(i, 2)), j + 1)

    def far_peer(j):
        i = j // 4
        return peer_at((n_z // 2 - (i + 1) // 2) * (1 - 2 * lax.rem(i, 2)), j)

    def greet(j, carry):
        pl.semaphore_signal(barrier, inc=1, device_id={"seq": near_peer(j)}, device_id_type=MESH)
        return carry

    lax.fori_loop(0, n_near, greet, 0)
    for peer in (f_right, f_left, mate):
        pl.semaphore_signal(barrier, inc=1, device_id={"fsdp": peer}, device_id_type=MESH)
    pl.semaphore_signal(barrier, inc=1, device_id={"canvas": other}, device_id_type=MESH)
    pl.semaphore_signal(barrier, inc=1, device_id={"seq": s_diag, "canvas": other}, device_id_type=MESH)

    col0 = pl.multiple_of(c * HALF, HALF)
    patch_load = pltpu.make_async_copy(patch_hbm.at[0, :, pl.ds(col0, HALF)], patch_v, load_sem.at[0])
    qkv_load = pltpu.make_async_copy(qkv_hbm, qkv_v, load_sem.at[1])
    out_load = pltpu.make_async_copy(out_hbm, out_v, load_sem.at[2])

    def rows_of(shard):
        return pl.ds(pl.multiple_of(shard * 128, 128), 128)

    up_load = pltpu.make_async_copy(up_hbm, up_v.at[rows_of(f)], load_sem.at[3])
    down_load = pltpu.make_async_copy(down_hbm, down_v.at[rows_of(f)], load_sem.at[4])
    index_loads = [
        pltpu.make_async_copy(keep_hbm, keep_ref, load_sem.at[5]),
        pltpu.make_async_copy(slot_hbm, slot_ref, load_sem.at[6]),
        pltpu.make_async_copy(freq_hbm, freq_ref, load_sem.at[7]),
        pltpu.make_async_copy(tile_hbm, tile_ref, load_sem.at[8]),
    ]
    for load in index_loads:
        load.start()
    for load in (patch_load, qkv_load, out_load, up_load, down_load):
        load.start()

    for load in index_loads:
        load.wait()
    slot = slot_ref[...]
    kept = keep_ref[...] == 1
    target = slot // 128
    lane4 = lax.rem(slot, 4)
    group = lax.rem(slot, 128) // 4
    first = jnp.where(kept & (lane4 == 0), target, -1)
    group_val = jnp.broadcast_to((group + 1).astype(F32), (8, 256)).astype(BF16)
    t_rows = lax.broadcasted_iota(jnp.int32, (128, 256), 0)
    hit = jnp.where(t_rows == first, 1.0, 0.0).astype(BF16)
    labels = matmul_nt(group_val, hit)
    lab_out[...] = labels[0:1, :]

    patch_load.wait()
    freq = freq_ref[...]
    within = lax.broadcasted_iota(jnp.int32, (16, QUART), 0)
    cell = jnp.where(c == 0, within // 4, lax.rem(within, 4))
    two_tiles = lax.broadcasted_iota(jnp.int32, (8, QUART), 0)

    def corner(t):
        tile = tile_ref[0, t]
        return jnp.where(c == 0, tile // 32, lax.rem(tile, 32)) * 4

    def embed(pair_at, carry):
        base = jnp.where(two_tiles < 4, corner(pair_at * 2), corner(pair_at * 2 + 1) - 4)
        angle = (base + two_tiles).astype(F32) * freq
        for quarter, table in enumerate((jnp.sin(angle), jnp.cos(angle))):
            for e in range(2):
                rows = pl.ds(pl.multiple_of(pair_at * 32 + e * 16, 16), 16)
                added = jnp.broadcast_to(table[e * 4:e * 4 + 1, :], (16, QUART))
                for k in range(1, 4):
                    added = jnp.where(cell == k, table[e * 4 + k:e * 4 + k + 1, :], added)
                tokens = patch_v[rows, quarter * QUART:(quarter + 1) * QUART].astype(F32)
                emb[quarter, rows, :] = (tokens + added).astype(BF16)
        return carry

    lax.fori_loop(0, 8, embed, 0)

    key = jnp.where(kept, target * 4 + lane4, -1000)
    row_i = lax.broadcasted_iota(jnp.int32, (512, QUART), 0)
    row_key = row_i // 8 * 4 + lax.rem(row_i, 4) + lax.rem(row_i // 4, 2) * 256
    pick0 = jnp.where(row_key == key, 1.0, 0.0).astype(BF16)
    pick1 = jnp.where(row_key == key + 256, 1.0, 0.0).astype(BF16)
    packed = matmul(pick0, emb[0]) + matmul(pick1, emb[1])
    send[...] = packed.astype(BF16).reshape(n_seq, 8, QUART)

    pl.semaphore_wait(barrier, n_near + 5)
    for dz in (n_z // 4, -(n_z // 4)):
        pl.semaphore_signal(met_sem, inc=1, device_id={"seq": peer_at(dz, 0)}, device_id_type=MESH)

    def push(to):
        block = lax.rem(to + n_seq - c, n_seq)
        pltpu.make_async_remote_copy(
            src_ref=lab_out, dst_ref=lab_in.at[s], send_sem=a2a_sem.at[0], recv_sem=a2a_sem.at[1],
            device_id={"seq": to}, device_id_type=MESH,
        ).start()
        pltpu.make_async_remote_copy(
            src_ref=send.at[block], dst_ref=recv.at[s], send_sem=a2a_sem.at[2], recv_sem=a2a_sem.at[3],
            device_id={"seq": to}, device_id_type=MESH,
        ).start()

    def push_near(j, carry):
        push(near_peer(j))
        return carry

    def push_far(j, carry):
        push(far_peer(j))
        return carry

    lax.fori_loop(0, n_near, push_near, 0)
    own_label = pltpu.make_async_copy(lab_out, lab_in.at[s], a2a_sem.at[4])
    own_label.start()
    own_rows = pltpu.make_async_copy(send.at[block_in], recv.at[s], a2a_sem.at[5])
    own_rows.start()

    def piece(buf, shard, part):
        first_row, count = ((0, 64), (64, 64), (0, 128))[part]
        return buf.at[pl.ds(pl.multiple_of(shard * 128 + first_row, 64), count)]

    shipped = []

    def ship(buf, shard, part, to, index_r):
        copy = pltpu.make_async_remote_copy(
            src_ref=piece(buf, shard, part), dst_ref=piece(buf, shard, part),
            send_sem=w_ssem.at[len(shipped)], recv_sem=w_rsem.at[index_r],
            device_id={"fsdp": to}, device_id_type=MESH,
        )
        copy.start()
        shipped.append(copy)

    def landed(buf, shard, part, index_r):
        view = piece(buf, shard, part)
        pltpu.make_async_copy(view, view, w_rsem.at[index_r]).wait()

    up_load.wait()
    ship(up_v, f, 2, f_right, 0)
    ship(up_v, f, 2, f_left, 1)
    ship(up_v, f, 2, mate, 10)
    down_load.wait()
    ship(down_v, f, 0, f_right, 2)
    ship(down_v, f, 1, f_left, 5)
    ship(down_v, f, 2, mate, 11)

    pl.semaphore_wait(met_sem, 2)
    lax.fori_loop(0, n_far, push_far, 0)

    own_label.wait()
    pltpu.make_async_copy(lab_in.at[pl.ds(0, n_seq - 1)], lab_in.at[pl.ds(0, n_seq - 1)], a2a_sem.at[1]).wait()
    lane_of = lax.broadcasted_iota(jnp.int32, (8, 128), 1)
    mine = jnp.where(lane_of == block_in, 1.0, 0.0).astype(BF16)
    came = matmul_nt(mine, lab_in[...].reshape(n_seq, 128).astype(BF16))
    spread_r = lax.broadcasted_iota(jnp.int32, (n_seq, 512), 0)
    spread_c = lax.broadcasted_iota(jnp.int32, (n_seq, 512), 1)
    spread = jnp.where(spread_r == spread_c // 8, 1.0, 0.0).astype(BF16)
    label_of = matmul(came.astype(BF16), spread).astype(jnp.int32)
    col_i = lax.broadcasted_iota(jnp.int32, (8, 512), 1)
    row_of = label_of * 4 - 4 + lax.rem(col_i, 4)
    half_of = lax.rem(col_i // 4, 2)
    r_i = lax.broadcasted_iota(jnp.int32, (128, 512), 0)
    places = []
    for h in range(2):
        row_h = jnp.where(half_of == h, row_of, -1)[0:1, :]
        places.append(jnp.where(r_i == row_h, 1.0, 0.0).astype(BF16))
    landed(up_v, f_left, 2, 0)
    ship(up_v, f_left, 0, f_right, 6)
    landed(up_v, f_right, 2, 1)
    ship(up_v, f_right, 1, f_left, 7)
    ship(down_v, f, 1, f_right, 3)
    ship(down_v, f, 0, f_left, 4)

    own_rows.wait()
    pltpu.make_async_copy(recv.at[pl.ds(0, n_seq - 1)], recv.at[pl.ds(0, n_seq - 1)], a2a_sem.at[3]).wait()
    came_rows = recv[...].reshape(512, QUART)
    size = 128 // chunks

    def view_of(block, half, k):
        return vis.at[block, half, pl.ds(k * size, size), :]

    def pass_on(block, half, to_block, k, to, leg):
        pltpu.make_async_remote_copy(
            src_ref=view_of(block, half, k), dst_ref=view_of(to_block, half, k),
            send_sem=vis_ssem.at[leg * chunks + k], recv_sem=vis_rsem.at[leg * chunks + k],
            device_id=to, device_id_type=MESH,
        ).start()

    def arrived(block, half, k, leg):
        view = view_of(block, half, k)
        pltpu.make_async_copy(view, view, vis_rsem.at[leg * chunks + k]).wait()

    def sent(k, leg):
        view = view_of(0, 0, k)
        pltpu.make_async_copy(view, view, vis_ssem.at[leg * chunks + k]).wait()

    pair = {"canvas": other}
    diagonal = {"seq": s_diag, "canvas": other}
    for k in range(chunks):
        for h in range(2):
            place = places[h][k * size:(k + 1) * size, :]
            vis[c, c, k * size:(k + 1) * size, h * QUART:(h + 1) * QUART] = matmul(place, came_rows).astype(BF16)
        pass_on(c, c, c, k, pair, 0)
    ship(up_v, f_left, 2, mate, 12)
    ship(up_v, f_right, 2, mate, 13)
    for k in range(chunks):
        arrived(other, other, k, 0)
        pass_on(other, other, c, k, diagonal, 1)
    for k in range(chunks):
        arrived(other, c, k, 1)
        pass_on(other, c, other, k, pair, 2)

    qkv_load.wait()

    def project(block):
        rows = pl.ds(pl.multiple_of(block * 128, 128), 128)
        normed[...] = normalised(jnp.concatenate([vis[block, 0], vis[block, 1]], axis=1).astype(F32)).astype(BF16)
        k_s[rows, :] = matmul(normed[...], qkv_v[1]).astype(BF16)
        v_s[rows, :] = matmul(normed[...], qkv_v[2]).astype(BF16)

        @pl.when(block == 0)
        def _():
            q_s[...] = matmul(normed[...], qkv_v[0]).astype(BF16)

    project(other)
    landed(up_v, f_far, 0, 6)
    landed(up_v, f_far, 1, 7)
    ship(up_v, f_far, 2, mate, 16)
    landed(down_v, f_left, 0, 2)
    ship(down_v, f_left, 0, f_right, 8)
    landed(down_v, f_right, 1, 5)
    ship(down_v, f_right, 1, f_left, 9)
    for k in range(chunks):
        arrived(c, other, k, 2)
    project(c)

    low = lax.broadcasted_iota(jnp.int32, (128, 128), 1) < 64
    att_copies = []
    for p in range(4):
        lanes = pl.ds(p * 128, 128)
        q_pair, k_pair, v_pair = q_s[:, lanes], k_s[:, lanes], v_s[:, lanes]
        mixed = []
        for e in range(2):
            q_one = jnp.where(low == (e == 0), q_pair.astype(F32), 0.0).astype(BF16)
            scores = matmul_nt(q_one, k_pair) * 0.125
            expo = jnp.exp(scores - jnp.max(scores, axis=-1, keepdims=True))
            total = jnp.sum(expo, axis=-1, keepdims=True)
            mixed.append(matmul(expo.astype(BF16), v_pair) / total)
        att[c, p] = jnp.where(low, mixed[0], mixed[1]).astype(BF16)
        copy = pltpu.make_async_remote_copy(
            src_ref=att.at[c, p], dst_ref=att.at[c, p], send_sem=att_sem.at[p], recv_sem=att_sem.at[4 + p],
            device_id=pair, device_id_type=MESH,
        )
        copy.start()
        att_copies.append(copy)

    landed(down_v, f_left, 1, 3)
    ship(down_v, f_left, 2, mate, 14)
    landed(down_v, f_right, 0, 4)
    ship(down_v, f_right, 2, mate, 15)

    out_load.wait()

    def mix(half):
        rows = pl.ds(pl.multiple_of(half * HALF, HALF), HALF)
        heads = jnp.concatenate([att[half, p] for p in range(4)], axis=1)
        return matmul(heads, out_v[rows, :])

    visible = jnp.concatenate([vis[0, 0], vis[0, 1]], axis=1).astype(F32)
    resid[...] = visible + mix(c)
    for copy in att_copies:
        copy.wait_recv()
    resid[...] += mix(other)
    normed2[...] = normalised(resid[...]).astype(BF16)

    landed(up_v, mate, 2, 10)
    landed(up_v, m_left, 2, 12)
    landed(up_v, m_right, 2, 13)
    landed(up_v, m_far, 2, 16)

    def widen(n, carry):
        cols = pl.ds(pl.multiple_of(n * 256, 256), 256)
        hidden[:, cols] = gelu(matmul(normed2[...], up_v[:, cols])).astype(BF16)
        return carry

    lax.fori_loop(0, 8, widen, 0)

    landed(down_v, f_far, 0, 8)
    landed(down_v, f_far, 1, 9)
    ship(down_v, f_far, 2, mate, 17)

    here = pl.ds(pl.multiple_of(c * 64, 64), 64)
    there = pl.ds(pl.multiple_of(other * 64, 64), 64)
    chip = f // 2
    y_copies = []
    for n, (step, shard, index_r) in enumerate(((0, mate, 11), (3, m_left, 14), (1, m_right, 15), (2, m_far, 17))):
        landed(down_v, shard, 2, index_r)
        cols = pl.ds(pl.multiple_of(lax.rem(chip + step, 4) * 256, 256), 256)
        part[:, cols] = matmul_nt(hidden[...], down_v[cols, :])
        y_out[n] = part[there, cols].astype(BF16)
        copy = pltpu.make_async_remote_copy(
            src_ref=y_out.at[n], dst_ref=y_in.at[n], send_sem=y_ssem.at[n], recv_sem=y_rsem.at[n],
            device_id=pair, device_id_type=MESH,
        )
        copy.start()
        y_copies.append(copy)
    for n, step in enumerate((0, 3, 1, 2)):
        cols = pl.ds(pl.multiple_of(lax.rem(chip + step, 4) * 256, 256), 256)
        y_copies[n].wait_recv()
        y_ref[:, cols] = (resid[here, cols] + part[here, cols] + y_in[n].astype(F32)).astype(BF16)

    first63 = pl.ds(0, n_seq - 1)
    pltpu.make_async_copy(lab_in.at[first63], lab_in.at[first63], a2a_sem.at[0]).wait()
    pltpu.make_async_copy(send.at[first63], send.at[first63], a2a_sem.at[2]).wait()
    for leg in range(3):
        for k in range(chunks):
            sent(k, leg)
    for copy in shipped:
        copy.wait_send()
    for copy in att_copies + y_copies:
        copy.wait_send()


def shards(chunks, patch_tokens, keep_mask, slot_index, tile_map, qkv_proj, out_proj, up_proj, down_proj):
    n_seq = lax.axis_size("seq")
    freq = jnp.asarray((10000.0 ** (-np.arange(QUART) / QUART)).astype(np.float32)).reshape(1, QUART)
    qkv = jnp.transpose(qkv_proj, (1, 2, 0, 3)).reshape(3, D, HALF)
    hbm = pl.BlockSpec(memory_space=pltpu.HBM)
    vmem = pl.BlockSpec(memory_space=pltpu.VMEM)
    y = pl.pallas_call(
        functools.partial(kernel, n_seq, chunks),
        name="encoder_layer",
        out_shape=pltpu.VMEM((64, D), BF16),
        in_specs=[hbm] * 9,
        out_specs=vmem,
        scratch_shapes=[
            pltpu.SMEM((1, 16), jnp.int32),
            pltpu.VMEM((1, 256), jnp.int32),
            pltpu.VMEM((1, 256), jnp.int32),
            pltpu.VMEM((1, QUART), F32),
            pltpu.VMEM((256, HALF), BF16),
            pltpu.VMEM((3, D, HALF), BF16),
            pltpu.VMEM((D, D), BF16),
            pltpu.VMEM((D, 2048), BF16),
            pltpu.VMEM((D, 2048), BF16),
            pltpu.VMEM((2, 256, QUART), BF16),
            pltpu.VMEM((n_seq, 8, QUART), BF16),
            pltpu.VMEM((n_seq, 8, QUART), BF16),
            pltpu.VMEM((1, 128), F32),
            pltpu.VMEM((n_seq, 1, 128), F32),
            pltpu.VMEM((2, 2, 128, HALF), BF16),
            pltpu.VMEM((128, D), BF16),
            pltpu.VMEM((128, HALF), BF16),
            pltpu.VMEM((256, HALF), BF16),
            pltpu.VMEM((256, HALF), BF16),
            pltpu.VMEM((2, 4, 128, 128), BF16),
            pltpu.VMEM((128, D), F32),
            pltpu.VMEM((128, D), BF16),
            pltpu.VMEM((128, 2048), BF16),
            pltpu.VMEM((128, D), F32),
            pltpu.VMEM((4, 64, 256), BF16),
            pltpu.VMEM((4, 64, 256), BF16),
            pltpu.SemaphoreType.REGULAR,
            pltpu.SemaphoreType.DMA((9,)),
            pltpu.SemaphoreType.DMA((6,)),
            pltpu.SemaphoreType.DMA((3 * chunks,)),
            pltpu.SemaphoreType.DMA((3 * chunks,)),
            pltpu.SemaphoreType.DMA((18,)),
            pltpu.SemaphoreType.DMA((18,)),
            pltpu.SemaphoreType.DMA((8,)),
            pltpu.SemaphoreType.DMA((4,)),
            pltpu.SemaphoreType.DMA((4,)),
        ],
        compiler_params=pltpu.CompilerParams(
            collective_id=0, has_side_effects=True, vmem_limit_bytes=58 * 1024 * 1024
        ),
    )(*[
        pltpu.with_memory_space_constraint(operand, pltpu.HBM)
        for operand in (tile_map, keep_mask, slot_index, freq, patch_tokens, qkv, out_proj, up_proj, down_proj)
    ])
    return y[None]


def solution(mesh):
    placed = (
        P("fsdp", "seq", None),
        P("fsdp", "seq"),
        P("fsdp", "seq"),
        P("fsdp", "seq"),
        P(None, "canvas", None, None),
        P(),
        P("fsdp", "canvas"),
        P("fsdp", "canvas"),
    )
    return jax.shard_map(
        functools.partial(shards, 4),
        mesh=mesh,
        in_specs=placed,
        out_specs=P("fsdp", ("seq", "canvas"), None),
        check_vma=False,
    )
```

```python
import functools

import jax
import jax.numpy as jnp
import numpy as np
from jax import lax
from jax.experimental import pallas as pl
from jax.experimental.pallas import tpu as pltpu
from jax.sharding import PartitionSpec as P

D = 1024
HALF = 512
QUART = 256
EPS = 1e-06
MESH = pl.DeviceIdType.MESH
F32 = jnp.float32
BF16 = jnp.bfloat16


def normalised(values):
    centered = values - jnp.mean(values, axis=-1, keepdims=True)
    spread = jnp.mean(centered * centered, axis=-1, keepdims=True)
    return centered * lax.rsqrt(spread + EPS)


def matmul(left, right):
    return jnp.dot(left, right, preferred_element_type=F32)


def matmul_nt(left, right):
    return lax.dot_general(left, right, (((1,), (1,)), ((), ())), preferred_element_type=F32)


def gelu(x):
    return 0.5 * x * (1.0 + lax.erf(x * (0.5**0.5)))


def kernel(
    n_seq, chunks,
    tile_hbm, keep_hbm, slot_hbm, freq_hbm, patch_hbm, qkv_hbm, out_hbm, up_hbm, down_hbm,
    y_ref,
    tile_ref, keep_ref, slot_ref, freq_ref, patch_v, qkv_v, out_v, up_v, down_v,
    emb, send, mid, recv, lab_out, lab_mid, lab_in, vis, normed, q_s, k_s, v_s, att, resid, normed2, hidden, part, y_out, y_in,
    met_sem, load_sem, a2a_sem, y_sem, vis_ssem, vis_rsem, w_ssem, w_rsem, att_sem, y_ssem, y_rsem,
):
    s = lax.axis_index("seq")
    f = lax.axis_index("fsdp")
    c = lax.axis_index("canvas")
    other = 1 - c
    f_right, f_left, f_far = lax.rem(f + 2, 8), lax.rem(f + 6, 8), lax.rem(f + 4, 8)
    mate = f + 1 - 2 * lax.rem(f, 2)
    m_right, m_left, m_far = lax.rem(mate + 2, 8), lax.rem(mate + 6, 8), lax.rem(mate + 4, 8)
    block_in = lax.rem(s + n_seq - c, n_seq)
    s_diag = lax.rem(s + n_seq + 2 * c - 1, n_seq)

    barrier = pltpu.get_barrier_semaphore()
    n_z = n_seq // 4
    z, y_hi = s // 4, lax.rem(s, 4)

    def peer_at(dz, dy):
        return lax.rem(z + dz + n_z, n_z) * 4 + lax.rem(y_hi + dy, 4)

    def far_first(j, reach):
        return (reach - (j + 1) // 2) * (1 - 2 * lax.rem(j, 2))

    for dy in (2, 1, 3):
        pl.semaphore_signal(barrier, inc=1, device_id={"seq": peer_at(0, dy)}, device_id_type=MESH)

    def greet(j, carry):
        dz = (n_z // 4 - j // 2) * (1 - 2 * lax.rem(j, 2))
        pl.semaphore_signal(barrier, inc=1, device_id={"seq": peer_at(dz, 0)}, device_id_type=MESH)
        return carry

    lax.fori_loop(0, n_z // 2, greet, 0)
    for peer in (f_right, f_left, mate):
        pl.semaphore_signal(barrier, inc=1, device_id={"fsdp": peer}, device_id_type=MESH)
    pl.semaphore_signal(barrier, inc=1, device_id={"canvas": other}, device_id_type=MESH)
    pl.semaphore_signal(barrier, inc=1, device_id={"seq": s_diag, "canvas": other}, device_id_type=MESH)

    col0 = pl.multiple_of(c * HALF, HALF)
    patch_load = pltpu.make_async_copy(patch_hbm.at[0, :, pl.ds(col0, HALF)], patch_v, load_sem.at[0])
    qkv_load = pltpu.make_async_copy(qkv_hbm, qkv_v, load_sem.at[1])
    out_load = pltpu.make_async_copy(out_hbm, out_v, load_sem.at[2])

    def rows_of(shard):
        return pl.ds(pl.multiple_of(shard * 128, 128), 128)

    up_load = pltpu.make_async_copy(up_hbm, up_v.at[rows_of(f)], load_sem.at[3])
    down_load = pltpu.make_async_copy(down_hbm, down_v.at[rows_of(f)], load_sem.at[4])
    index_loads = [
        pltpu.make_async_copy(keep_hbm, keep_ref, load_sem.at[5]),
        pltpu.make_async_copy(slot_hbm, slot_ref, load_sem.at[6]),
        pltpu.make_async_copy(freq_hbm, freq_ref, load_sem.at[7]),
        pltpu.make_async_copy(tile_hbm, tile_ref, load_sem.at[8]),
    ]
    for load in index_loads:
        load.start()
    for load in (patch_load, qkv_load, out_load, up_load, down_load):
        load.start()

    for load in index_loads:
        load.wait()
    slot = slot_ref[...]
    kept = keep_ref[...] == 1
    target = slot // 128
    lane4 = lax.rem(slot, 4)
    group = lax.rem(slot, 128) // 4
    first = jnp.where(kept & (lane4 == 0), target, -1)
    group_val = jnp.broadcast_to((group + 1).astype(F32), (8, 256)).astype(BF16)
    t_rows = lax.broadcasted_iota(jnp.int32, (128, 256), 0)
    hit = jnp.where(t_rows == first, 1.0, 0.0).astype(BF16)
    labels = matmul_nt(group_val, hit)
    lab_out[...] = labels[0:1, :]

    patch_load.wait()
    freq = freq_ref[...]
    within = lax.broadcasted_iota(jnp.int32, (16, QUART), 0)
    cell = jnp.where(c == 0, within // 4, lax.rem(within, 4))
    two_tiles = lax.broadcasted_iota(jnp.int32, (8, QUART), 0)

    def corner(t):
        tile = tile_ref[0, t]
        return jnp.where(c == 0, tile // 32, lax.rem(tile, 32)) * 4

    def embed(pair_at, carry):
        base = jnp.where(two_tiles < 4, corner(pair_at * 2), corner(pair_at * 2 + 1) - 4)
        angle = (base + two_tiles).astype(F32) * freq
        for quarter, table in enumerate((jnp.sin(angle), jnp.cos(angle))):
            for e in range(2):
                rows = pl.ds(pl.multiple_of(pair_at * 32 + e * 16, 16), 16)
                added = jnp.broadcast_to(table[e * 4:e * 4 + 1, :], (16, QUART))
                for k in range(1, 4):
                    added = jnp.where(cell == k, table[e * 4 + k:e * 4 + k + 1, :], added)
                tokens = patch_v[rows, quarter * QUART:(quarter + 1) * QUART].astype(F32)
                emb[quarter, rows, :] = (tokens + added).astype(BF16)
        return carry

    lax.fori_loop(0, 8, embed, 0)

    key = jnp.where(kept, target * 4 + lane4, -1000)
    row_i = lax.broadcasted_iota(jnp.int32, (512, QUART), 0)
    slot_i = row_i // 8
    block_i = lax.rem(lax.rem(slot_i, n_z) * 4 + slot_i // n_z + n_seq - c, n_seq)
    row_key = block_i * 4 + lax.rem(row_i, 4) + lax.rem(row_i // 4, 2) * 256
    pick0 = jnp.where(row_key == key, 1.0, 0.0).astype(BF16)
    pick1 = jnp.where(row_key == key + 256, 1.0, 0.0).astype(BF16)
    packed = matmul(pick0, emb[0]) + matmul(pick1, emb[1])
    send[...] = packed.astype(BF16).reshape(4, n_z, 8, QUART)

    pl.semaphore_wait(barrier, n_z // 2 + 8)
    for dz in (n_z // 4, -(n_z // 4)):
        pl.semaphore_signal(met_sem, inc=1, device_id={"seq": peer_at(dz, 0)}, device_id_type=MESH)

    own_label = pltpu.make_async_copy(lab_out, lab_mid.at[y_hi], a2a_sem.at[4])
    own_label.start()
    own_rows = pltpu.make_async_copy(send.at[y_hi], mid.at[y_hi], a2a_sem.at[5])
    own_rows.start()
    for dy in (2, 1, 3):
        pltpu.make_async_remote_copy(
            src_ref=lab_out, dst_ref=lab_mid.at[y_hi], send_sem=a2a_sem.at[0], recv_sem=a2a_sem.at[1],
            device_id={"seq": peer_at(0, dy)}, device_id_type=MESH,
        ).start()
    n_part = n_z // 4
    parts = [lax.rem(z // n_part + off, 4) for off in (2, 3, 1, 0)]
    for q in parts:
        column = pl.ds(q * n_part, n_part)
        for dy in (2, 1, 3):
            pltpu.make_async_remote_copy(
                src_ref=send.at[lax.rem(y_hi + dy, 4), column], dst_ref=mid.at[y_hi, column],
                send_sem=a2a_sem.at[2], recv_sem=y_sem.at[q],
                device_id={"seq": peer_at(0, dy)}, device_id_type=MESH,
            ).start()

    def piece(buf, shard, part):
        first_row, count = ((0, 64), (64, 64), (0, 128))[part]
        return buf.at[pl.ds(pl.multiple_of(shard * 128 + first_row, 64), count)]

    shipped = []

    def ship(buf, shard, part, to, index_r):
        copy = pltpu.make_async_remote_copy(
            src_ref=piece(buf, shard, part), dst_ref=piece(buf, shard, part),
            send_sem=w_ssem.at[len(shipped)], recv_sem=w_rsem.at[index_r],
            device_id={"fsdp": to}, device_id_type=MESH,
        )
        copy.start()
        shipped.append(copy)

    def landed(buf, shard, part, index_r):
        view = piece(buf, shard, part)
        pltpu.make_async_copy(view, view, w_rsem.at[index_r]).wait()

    up_load.wait()
    ship(up_v, f, 2, f_right, 0)
    ship(up_v, f, 2, f_left, 1)
    ship(up_v, f, 2, mate, 10)
    down_load.wait()
    ship(down_v, f, 0, f_right, 2)
    ship(down_v, f, 1, f_left, 5)
    ship(down_v, f, 2, mate, 11)

    pl.semaphore_wait(met_sem, 2)
    own_label.wait()
    three = pl.ds(0, 3)
    pltpu.make_async_copy(lab_mid.at[three], lab_mid.at[three], a2a_sem.at[1]).wait()
    own_labels = pltpu.make_async_copy(lab_mid, lab_in.at[z], a2a_sem.at[8])
    own_labels.start()

    def push_labels(j, carry):
        pltpu.make_async_remote_copy(
            src_ref=lab_mid, dst_ref=lab_in.at[z], send_sem=a2a_sem.at[6], recv_sem=a2a_sem.at[7],
            device_id={"seq": peer_at(far_first(j, n_z // 2), 0)}, device_id_type=MESH,
        ).start()
        return carry

    lax.fori_loop(0, n_z - 1, push_labels, 0)
    own_rows.wait()
    for q in parts:
        came = mid.at[three, pl.ds(q * n_part, n_part)]
        pltpu.make_async_copy(came, came, y_sem.at[q]).wait()
        for j in range(n_part):
            to = q * n_part + j

            @pl.when(to != z)
            def _():
                pltpu.make_async_remote_copy(
                    src_ref=mid.at[:, to], dst_ref=recv.at[z], send_sem=a2a_sem.at[9], recv_sem=a2a_sem.at[3],
                    device_id={"seq": to * 4 + y_hi}, device_id_type=MESH,
                ).start()

    own_column = pltpu.make_async_copy(mid.at[:, z], recv.at[z], a2a_sem.at[10])
    own_column.start()

    others = pl.ds(0, n_z - 1)
    own_labels.wait()
    pltpu.make_async_copy(lab_in.at[others], lab_in.at[others], a2a_sem.at[7]).wait()
    lane_of = lax.broadcasted_iota(jnp.int32, (8, 128), 1)
    mine = jnp.where(lane_of == block_in, 1.0, 0.0).astype(BF16)
    came = matmul_nt(mine, lab_in[...].reshape(n_seq, 128).astype(BF16))
    spread_r = lax.broadcasted_iota(jnp.int32, (n_seq, 512), 0)
    spread_c = lax.broadcasted_iota(jnp.int32, (n_seq, 512), 1)
    spread = jnp.where(spread_r == spread_c // 8, 1.0, 0.0).astype(BF16)
    label_of = matmul(came.astype(BF16), spread).astype(jnp.int32)
    col_i = lax.broadcasted_iota(jnp.int32, (8, 512), 1)
    row_of = label_of * 4 - 4 + lax.rem(col_i, 4)
    half_of = lax.rem(col_i // 4, 2)
    r_i = lax.broadcasted_iota(jnp.int32, (128, 512), 0)
    places = []
    for h in range(2):
        row_h = jnp.where(half_of == h, row_of, -1)[0:1, :]
        places.append(jnp.where(r_i == row_h, 1.0, 0.0).astype(BF16))
    landed(up_v, f_left, 2, 0)
    ship(up_v, f_left, 0, f_right, 6)
    landed(up_v, f_right, 2, 1)
    ship(up_v, f_right, 1, f_left, 7)
    ship(down_v, f, 1, f_right, 3)
    ship(down_v, f, 0, f_left, 4)

    own_column.wait()
    pltpu.make_async_copy(recv.at[others], recv.at[others], a2a_sem.at[3]).wait()
    came_rows = recv[...].reshape(512, QUART)
    size = 128 // chunks

    def view_of(block, half, k):
        return vis.at[block, half, pl.ds(k * size, size), :]

    def pass_on(block, half, to_block, k, to, leg):
        pltpu.make_async_remote_copy(
            src_ref=view_of(block, half, k), dst_ref=view_of(to_block, half, k),
            send_sem=vis_ssem.at[leg * chunks + k], recv_sem=vis_rsem.at[leg * chunks + k],
            device_id=to, device_id_type=MESH,
        ).start()

    def arrived(block, half, k, leg):
        view = view_of(block, half, k)
        pltpu.make_async_copy(view, view, vis_rsem.at[leg * chunks + k]).wait()

    def sent(k, leg):
        view = view_of(0, 0, k)
        pltpu.make_async_copy(view, view, vis_ssem.at[leg * chunks + k]).wait()

    pair = {"canvas": other}
    diagonal = {"seq": s_diag, "canvas": other}
    for k in range(chunks):
        for h in range(2):
            place = places[h][k * size:(k + 1) * size, :]
            vis[c, c, k * size:(k + 1) * size, h * QUART:(h + 1) * QUART] = matmul(place, came_rows).astype(BF16)
        pass_on(c, c, c, k, pair, 0)
    ship(up_v, f_left, 2, mate, 12)
    ship(up_v, f_right, 2, mate, 13)
    for k in range(chunks):
        arrived(other, other, k, 0)
        pass_on(other, other, c, k, diagonal, 1)
    for k in range(chunks):
        arrived(other, c, k, 1)
        pass_on(other, c, other, k, pair, 2)

    qkv_load.wait()

    def project(block):
        rows = pl.ds(pl.multiple_of(block * 128, 128), 128)
        normed[...] = normalised(jnp.concatenate([vis[block, 0], vis[block, 1]], axis=1).astype(F32)).astype(BF16)
        k_s[rows, :] = matmul(normed[...], qkv_v[1]).astype(BF16)
        v_s[rows, :] = matmul(normed[...], qkv_v[2]).astype(BF16)

        @pl.when(block == 0)
        def _():
            q_s[...] = matmul(normed[...], qkv_v[0]).astype(BF16)

    project(other)
    landed(up_v, f_far, 0, 6)
    landed(up_v, f_far, 1, 7)
    ship(up_v, f_far, 2, mate, 16)
    landed(down_v, f_left, 0, 2)
    ship(down_v, f_left, 0, f_right, 8)
    landed(down_v, f_right, 1, 5)
    ship(down_v, f_right, 1, f_left, 9)
    for k in range(chunks):
        arrived(c, other, k, 2)
    project(c)

    low = lax.broadcasted_iota(jnp.int32, (128, 128), 1) < 64
    att_copies = []
    for p in range(4):
        lanes = pl.ds(p * 128, 128)
        q_pair, k_pair, v_pair = q_s[:, lanes], k_s[:, lanes], v_s[:, lanes]
        mixed = []
        for e in range(2):
            q_one = jnp.where(low == (e == 0), q_pair.astype(F32), 0.0).astype(BF16)
            scores = matmul_nt(q_one, k_pair) * 0.125
            expo = jnp.exp(scores - jnp.max(scores, axis=-1, keepdims=True))
            total = jnp.sum(expo, axis=-1, keepdims=True)
            mixed.append(matmul(expo.astype(BF16), v_pair) / total)
        att[c, p] = jnp.where(low, mixed[0], mixed[1]).astype(BF16)
        copy = pltpu.make_async_remote_copy(
            src_ref=att.at[c, p], dst_ref=att.at[c, p], send_sem=att_sem.at[p], recv_sem=att_sem.at[4 + p],
            device_id=pair, device_id_type=MESH,
        )
        copy.start()
        att_copies.append(copy)

    landed(down_v, f_left, 1, 3)
    ship(down_v, f_left, 2, mate, 14)
    landed(down_v, f_right, 0, 4)
    ship(down_v, f_right, 2, mate, 15)

    out_load.wait()

    def mix(half):
        rows = pl.ds(pl.multiple_of(half * HALF, HALF), HALF)
        heads = jnp.concatenate([att[half, p] for p in range(4)], axis=1)
        return matmul(heads, out_v[rows, :])

    visible = jnp.concatenate([vis[0, 0], vis[0, 1]], axis=1).astype(F32)
    resid[...] = visible + mix(c)
    for copy in att_copies:
        copy.wait_recv()
    resid[...] += mix(other)
    normed2[...] = normalised(resid[...]).astype(BF16)

    landed(up_v, mate, 2, 10)
    landed(up_v, m_left, 2, 12)
    landed(up_v, m_right, 2, 13)
    landed(up_v, m_far, 2, 16)

    def widen(n, carry):
        cols = pl.ds(pl.multiple_of(n * 256, 256), 256)
        hidden[:, cols] = gelu(matmul(normed2[...], up_v[:, cols])).astype(BF16)
        return carry

    lax.fori_loop(0, 8, widen, 0)

    landed(down_v, f_far, 0, 8)
    landed(down_v, f_far, 1, 9)
    ship(down_v, f_far, 2, mate, 17)

    here = pl.ds(pl.multiple_of(c * 64, 64), 64)
    there = pl.ds(pl.multiple_of(other * 64, 64), 64)
    chip = f // 2
    y_copies = []
    for n, (step, shard, index_r) in enumerate(((0, mate, 11), (3, m_left, 14), (1, m_right, 15), (2, m_far, 17))):
        landed(down_v, shard, 2, index_r)
        cols = pl.ds(pl.multiple_of(lax.rem(chip + step, 4) * 256, 256), 256)
        part[:, cols] = matmul_nt(hidden[...], down_v[cols, :])
        y_out[n] = part[there, cols].astype(BF16)
        copy = pltpu.make_async_remote_copy(
            src_ref=y_out.at[n], dst_ref=y_in.at[n], send_sem=y_ssem.at[n], recv_sem=y_rsem.at[n],
            device_id=pair, device_id_type=MESH,
        )
        copy.start()
        y_copies.append(copy)
    for n, step in enumerate((0, 3, 1, 2)):
        cols = pl.ds(pl.multiple_of(lax.rem(chip + step, 4) * 256, 256), 256)
        y_copies[n].wait_recv()
        y_ref[:, cols] = (resid[here, cols] + part[here, cols] + y_in[n].astype(F32)).astype(BF16)

    pltpu.make_async_copy(lab_mid.at[three], lab_mid.at[three], a2a_sem.at[0]).wait()
    pltpu.make_async_copy(send.at[three], send.at[three], a2a_sem.at[2]).wait()
    pltpu.make_async_copy(lab_in.at[others], lab_in.at[others], a2a_sem.at[6]).wait()
    pltpu.make_async_copy(recv.at[others], recv.at[others], a2a_sem.at[9]).wait()
    for leg in range(3):
        for k in range(chunks):
            sent(k, leg)
    for copy in shipped:
        copy.wait_send()
    for copy in att_copies + y_copies:
        copy.wait_send()


def shards(chunks, patch_tokens, keep_mask, slot_index, tile_map, qkv_proj, out_proj, up_proj, down_proj):
    n_seq = lax.axis_size("seq")
    freq = jnp.asarray((10000.0 ** (-np.arange(QUART) / QUART)).astype(np.float32)).reshape(1, QUART)
    qkv = jnp.transpose(qkv_proj, (1, 2, 0, 3)).reshape(3, D, HALF)
    hbm = pl.BlockSpec(memory_space=pltpu.HBM)
    vmem = pl.BlockSpec(memory_space=pltpu.VMEM)
    y = pl.pallas_call(
        functools.partial(kernel, n_seq, chunks),
        name="encoder_layer",
        out_shape=pltpu.VMEM((64, D), BF16),
        in_specs=[hbm] * 9,
        out_specs=vmem,
        scratch_shapes=[
            pltpu.SMEM((1, 16), jnp.int32),
            pltpu.VMEM((1, 256), jnp.int32),
            pltpu.VMEM((1, 256), jnp.int32),
            pltpu.VMEM((1, QUART), F32),
            pltpu.VMEM((256, HALF), BF16),
            pltpu.VMEM((3, D, HALF), BF16),
            pltpu.VMEM((D, D), BF16),
            pltpu.VMEM((D, 2048), BF16),
            pltpu.VMEM((D, 2048), BF16),
            pltpu.VMEM((2, 256, QUART), BF16),
            pltpu.VMEM((4, n_seq // 4, 8, QUART), BF16),
            pltpu.VMEM((4, n_seq // 4, 8, QUART), BF16),
            pltpu.VMEM((n_seq // 4, 4, 8, QUART), BF16),
            pltpu.VMEM((1, 128), F32),
            pltpu.VMEM((4, 1, 128), F32),
            pltpu.VMEM((n_seq // 4, 4, 1, 128), F32),
            pltpu.VMEM((2, 2, 128, HALF), BF16),
            pltpu.VMEM((128, D), BF16),
            pltpu.VMEM((128, HALF), BF16),
            pltpu.VMEM((256, HALF), BF16),
            pltpu.VMEM((256, HALF), BF16),
            pltpu.VMEM((2, 4, 128, 128), BF16),
            pltpu.VMEM((128, D), F32),
            pltpu.VMEM((128, D), BF16),
            pltpu.VMEM((128, 2048), BF16),
            pltpu.VMEM((128, D), F32),
            pltpu.VMEM((4, 64, 256), BF16),
            pltpu.VMEM((4, 64, 256), BF16),
            pltpu.SemaphoreType.REGULAR,
            pltpu.SemaphoreType.DMA((9,)),
            pltpu.SemaphoreType.DMA((11,)),
            pltpu.SemaphoreType.DMA((4,)),
            pltpu.SemaphoreType.DMA((3 * chunks,)),
            pltpu.SemaphoreType.DMA((3 * chunks,)),
            pltpu.SemaphoreType.DMA((18,)),
            pltpu.SemaphoreType.DMA((18,)),
            pltpu.SemaphoreType.DMA((8,)),
            pltpu.SemaphoreType.DMA((4,)),
            pltpu.SemaphoreType.DMA((4,)),
        ],
        compiler_params=pltpu.CompilerParams(
            collective_id=0, has_side_effects=True, vmem_limit_bytes=58 * 1024 * 1024
        ),
    )(*[
        pltpu.with_memory_space_constraint(operand, pltpu.HBM)
        for operand in (tile_map, keep_mask, slot_index, freq, patch_tokens, qkv, out_proj, up_proj, down_proj)
    ])
    return y[None]


def solution(mesh):
    placed = (
        P("fsdp", "seq", None),
        P("fsdp", "seq"),
        P("fsdp", "seq"),
        P("fsdp", "seq"),
        P(None, "canvas", None, None),
        P(),
        P("fsdp", "canvas"),
        P("fsdp", "canvas"),
    )
    return jax.shard_map(
        functools.partial(shards, 4),
        mesh=mesh,
        in_specs=placed,
        out_specs=P("fsdp", ("seq", "canvas"), None),
        check_vma=False,
    )
```

```python
import functools

import jax
import jax.numpy as jnp
import numpy as np
from jax import lax
from jax.experimental import pallas as pl
from jax.experimental.pallas import tpu as pltpu
from jax.sharding import PartitionSpec as P

D = 1024
HALF = 512
QUART = 256
EPS = 1e-06
MESH = pl.DeviceIdType.MESH
F32 = jnp.float32
BF16 = jnp.bfloat16


def normalised(values):
    centered = values - jnp.mean(values, axis=-1, keepdims=True)
    spread = jnp.mean(centered * centered, axis=-1, keepdims=True)
    return centered * lax.rsqrt(spread + EPS)


def matmul(left, right):
    return jnp.dot(left, right, preferred_element_type=F32)


def matmul_nt(left, right):
    return lax.dot_general(left, right, (((1,), (1,)), ((), ())), preferred_element_type=F32)


def gelu(x):
    return 0.5 * x * (1.0 + lax.erf(x * (0.5**0.5)))


def kernel(
    n_seq, chunks,
    tile_hbm, keep_hbm, slot_hbm, freq_hbm, patch_hbm, qkv_hbm, out_hbm, up_hbm, down_hbm,
    y_ref,
    tile_ref, keep_ref, slot_ref, freq_ref, patch_v, qkv_v, out_v, up_v, down_v,
    emb, send, mid, recv, lab_out, lab_mid, lab_in, vis, normed, q_s, k_s, v_s, att, resid, normed2, hidden, part, y_out, y_in,
    met_sem, load_sem, a2a_sem, y_sem, vis_ssem, vis_rsem, w_ssem, w_rsem, att_sem, y_ssem, y_rsem,
):
    s = lax.axis_index("seq")
    f = lax.axis_index("fsdp")
    c = lax.axis_index("canvas")
    other = 1 - c
    f_right, f_left, f_far = lax.rem(f + 2, 8), lax.rem(f + 6, 8), lax.rem(f + 4, 8)
    mate = f + 1 - 2 * lax.rem(f, 2)
    m_right, m_left, m_far = lax.rem(mate + 2, 8), lax.rem(mate + 6, 8), lax.rem(mate + 4, 8)
    block_in = lax.rem(s + n_seq - c, n_seq)
    s_diag = lax.rem(s + n_seq + 2 * c - 1, n_seq)

    barrier = pltpu.get_barrier_semaphore()
    n_z = n_seq // 4
    z, y_hi = s // 4, lax.rem(s, 4)

    def peer_at(dz, dy):
        return lax.rem(z + dz + n_z, n_z) * 4 + lax.rem(y_hi + dy, 4)

    def far_first(j, reach):
        return (reach - (j + 1) // 2) * (1 - 2 * lax.rem(j, 2))

    for dy in (2, 1, 3):
        pl.semaphore_signal(barrier, inc=1, device_id={"seq": peer_at(0, dy)}, device_id_type=MESH)

    def greet(j, carry):
        dz = (n_z // 4 - j // 2) * (1 - 2 * lax.rem(j, 2))
        pl.semaphore_signal(barrier, inc=1, device_id={"seq": peer_at(dz, 0)}, device_id_type=MESH)
        return carry

    lax.fori_loop(0, n_z // 2, greet, 0)
    for peer in (f_right, f_left, mate):
        pl.semaphore_signal(barrier, inc=1, device_id={"fsdp": peer}, device_id_type=MESH)
    pl.semaphore_signal(barrier, inc=1, device_id={"canvas": other}, device_id_type=MESH)
    pl.semaphore_signal(barrier, inc=1, device_id={"seq": s_diag, "canvas": other}, device_id_type=MESH)

    col0 = pl.multiple_of(c * HALF, HALF)
    patch_load = pltpu.make_async_copy(patch_hbm.at[0, :, pl.ds(col0, HALF)], patch_v, load_sem.at[0])
    qkv_load = pltpu.make_async_copy(qkv_hbm, qkv_v, load_sem.at[1])
    out_load = pltpu.make_async_copy(out_hbm, out_v, load_sem.at[2])

    def rows_of(shard):
        return pl.ds(pl.multiple_of(shard * 128, 128), 128)

    up_load = pltpu.make_async_copy(up_hbm, up_v.at[rows_of(f)], load_sem.at[3])
    down_load = pltpu.make_async_copy(down_hbm, down_v.at[rows_of(f)], load_sem.at[4])
    index_loads = [
        pltpu.make_async_copy(keep_hbm, keep_ref, load_sem.at[5]),
        pltpu.make_async_copy(slot_hbm, slot_ref, load_sem.at[6]),
        pltpu.make_async_copy(freq_hbm, freq_ref, load_sem.at[7]),
        pltpu.make_async_copy(tile_hbm, tile_ref, load_sem.at[8]),
    ]
    for load in index_loads:
        load.start()
    patch_load.start()

    for load in index_loads:
        load.wait()
    slot = slot_ref[...]
    kept = keep_ref[...] == 1
    target = slot // 128
    lane4 = lax.rem(slot, 4)
    group = lax.rem(slot, 128) // 4
    first = jnp.where(kept & (lane4 == 0), target, -1)
    group_val = jnp.broadcast_to((group + 1).astype(F32), (8, 256)).astype(BF16)
    t_rows = lax.broadcasted_iota(jnp.int32, (128, 256), 0)
    hit = jnp.where(t_rows == first, 1.0, 0.0).astype(BF16)
    labels = matmul_nt(group_val, hit)
    lab_out[...] = labels[0:1, :]

    patch_load.wait()
    for load in (up_load, down_load, qkv_load, out_load):
        load.start()
    freq = freq_ref[...]
    within = lax.broadcasted_iota(jnp.int32, (16, QUART), 0)
    cell = jnp.where(c == 0, within // 4, lax.rem(within, 4))
    two_tiles = lax.broadcasted_iota(jnp.int32, (8, QUART), 0)

    def corner(t):
        tile = tile_ref[0, t]
        return jnp.where(c == 0, tile // 32, lax.rem(tile, 32)) * 4

    def embed(pair_at, carry):
        base = jnp.where(two_tiles < 4, corner(pair_at * 2), corner(pair_at * 2 + 1) - 4)
        angle = (base + two_tiles).astype(F32) * freq
        for quarter, table in enumerate((jnp.sin(angle), jnp.cos(angle))):
            for e in range(2):
                rows = pl.ds(pl.multiple_of(pair_at * 32 + e * 16, 16), 16)
                added = jnp.broadcast_to(table[e * 4:e * 4 + 1, :], (16, QUART))
                for k in range(1, 4):
                    added = jnp.where(cell == k, table[e * 4 + k:e * 4 + k + 1, :], added)
                tokens = patch_v[rows, quarter * QUART:(quarter + 1) * QUART].astype(F32)
                emb[quarter, rows, :] = (tokens + added).astype(BF16)
        return carry

    lax.fori_loop(0, 8, embed, 0)

    key = jnp.where(kept, target * 4 + lane4, -1000)
    row_i = lax.broadcasted_iota(jnp.int32, (512, QUART), 0)
    slot_i = row_i // 8
    block_i = lax.rem(lax.rem(slot_i, n_z) * 4 + slot_i // n_z + n_seq - c, n_seq)
    row_key = block_i * 4 + lax.rem(row_i, 4) + lax.rem(row_i // 4, 2) * 256
    pick0 = jnp.where(row_key == key, 1.0, 0.0).astype(BF16)
    pick1 = jnp.where(row_key == key + 256, 1.0, 0.0).astype(BF16)
    packed = matmul(pick0, emb[0]) + matmul(pick1, emb[1])
    send[...] = packed.astype(BF16).reshape(4, n_z, 8, QUART)

    pl.semaphore_wait(barrier, n_z // 2 + 8)
    for dz in (n_z // 4, -(n_z // 4)):
        pl.semaphore_signal(met_sem, inc=1, device_id={"seq": peer_at(dz, 0)}, device_id_type=MESH)

    own_label = pltpu.make_async_copy(lab_out, lab_mid.at[y_hi], a2a_sem.at[4])
    own_label.start()
    own_rows = pltpu.make_async_copy(send.at[y_hi], mid.at[y_hi], a2a_sem.at[5])
    own_rows.start()
    for dy in (2, 1, 3):
        pltpu.make_async_remote_copy(
            src_ref=lab_out, dst_ref=lab_mid.at[y_hi], send_sem=a2a_sem.at[0], recv_sem=a2a_sem.at[1],
            device_id={"seq": peer_at(0, dy)}, device_id_type=MESH,
        ).start()
    n_part = n_z // 4
    parts = [lax.rem(z // n_part + off, 4) for off in (2, 3, 1, 0)]
    for q in parts:
        column = pl.ds(q * n_part, n_part)
        for dy in (2, 1, 3):
            pltpu.make_async_remote_copy(
                src_ref=send.at[lax.rem(y_hi + dy, 4), column], dst_ref=mid.at[y_hi, column],
                send_sem=a2a_sem.at[2], recv_sem=y_sem.at[q],
                device_id={"seq": peer_at(0, dy)}, device_id_type=MESH,
            ).start()

    def piece(buf, shard, part):
        first_row, count = ((0, 64), (64, 64), (0, 128))[part]
        return buf.at[pl.ds(pl.multiple_of(shard * 128 + first_row, 64), count)]

    shipped = []

    def ship(buf, shard, part, to, index_r):
        copy = pltpu.make_async_remote_copy(
            src_ref=piece(buf, shard, part), dst_ref=piece(buf, shard, part),
            send_sem=w_ssem.at[len(shipped)], recv_sem=w_rsem.at[index_r],
            device_id={"fsdp": to}, device_id_type=MESH,
        )
        copy.start()
        shipped.append(copy)

    def landed(buf, shard, part, index_r):
        view = piece(buf, shard, part)
        pltpu.make_async_copy(view, view, w_rsem.at[index_r]).wait()

    up_load.wait()
    ship(up_v, f, 2, f_right, 0)
    ship(up_v, f, 2, f_left, 1)
    ship(up_v, f, 2, mate, 10)
    down_load.wait()
    ship(down_v, f, 0, f_right, 2)
    ship(down_v, f, 1, f_left, 5)
    ship(down_v, f, 2, mate, 11)

    pl.semaphore_wait(met_sem, 2)
    own_label.wait()
    three = pl.ds(0, 3)
    pltpu.make_async_copy(lab_mid.at[three], lab_mid.at[three], a2a_sem.at[1]).wait()
    own_labels = pltpu.make_async_copy(lab_mid, lab_in.at[z], a2a_sem.at[8])
    own_labels.start()

    def push_labels(j, carry):
        pltpu.make_async_remote_copy(
            src_ref=lab_mid, dst_ref=lab_in.at[z], send_sem=a2a_sem.at[6], recv_sem=a2a_sem.at[7],
            device_id={"seq": peer_at(far_first(j, n_z // 2), 0)}, device_id_type=MESH,
        ).start()
        return carry

    lax.fori_loop(0, n_z - 1, push_labels, 0)
    own_rows.wait()
    for q in parts:
        came = mid.at[three, pl.ds(q * n_part, n_part)]
        pltpu.make_async_copy(came, came, y_sem.at[q]).wait()
        for j in range(n_part):
            to = q * n_part + j

            @pl.when(to != z)
            def _():
                pltpu.make_async_remote_copy(
                    src_ref=mid.at[:, to], dst_ref=recv.at[z], send_sem=a2a_sem.at[9], recv_sem=a2a_sem.at[3],
                    device_id={"seq": to * 4 + y_hi}, device_id_type=MESH,
                ).start()

    own_column = pltpu.make_async_copy(mid.at[:, z], recv.at[z], a2a_sem.at[10])
    own_column.start()

    landed(up_v, f_left, 2, 0)
    ship(up_v, f_left, 0, f_right, 6)
    landed(up_v, f_right, 2, 1)
    ship(up_v, f_right, 1, f_left, 7)
    ship(down_v, f, 1, f_right, 3)
    ship(down_v, f, 0, f_left, 4)

    others = pl.ds(0, n_z - 1)
    own_labels.wait()
    pltpu.make_async_copy(lab_in.at[others], lab_in.at[others], a2a_sem.at[7]).wait()
    lane_of = lax.broadcasted_iota(jnp.int32, (8, 128), 1)
    mine = jnp.where(lane_of == block_in, 1.0, 0.0).astype(BF16)
    came = matmul_nt(mine, lab_in[...].reshape(n_seq, 128).astype(BF16))
    spread_r = lax.broadcasted_iota(jnp.int32, (n_seq, 512), 0)
    spread_c = lax.broadcasted_iota(jnp.int32, (n_seq, 512), 1)
    spread = jnp.where(spread_r == spread_c // 8, 1.0, 0.0).astype(BF16)
    label_of = matmul(came.astype(BF16), spread).astype(jnp.int32)
    col_i = lax.broadcasted_iota(jnp.int32, (8, 512), 1)
    row_of = label_of * 4 - 4 + lax.rem(col_i, 4)
    half_of = lax.rem(col_i // 4, 2)
    r_i = lax.broadcasted_iota(jnp.int32, (128, 512), 0)
    places = []
    for h in range(2):
        row_h = jnp.where(half_of == h, row_of, -1)[0:1, :]
        places.append(jnp.where(r_i == row_h, 1.0, 0.0).astype(BF16))
    places = jnp.concatenate(places, axis=0)
    own_column.wait()
    pltpu.make_async_copy(recv.at[others], recv.at[others], a2a_sem.at[3]).wait()
    came_rows = recv[...].reshape(512, QUART)
    size = 128 // chunks

    def view_of(block, half, k):
        return vis.at[block, half, pl.ds(k * size, size), :]

    def pass_on(block, half, to_block, k, to, leg):
        pltpu.make_async_remote_copy(
            src_ref=view_of(block, half, k), dst_ref=view_of(to_block, half, k),
            send_sem=vis_ssem.at[leg * chunks + k], recv_sem=vis_rsem.at[leg * chunks + k],
            device_id=to, device_id_type=MESH,
        ).start()

    def arrived(block, half, k, leg):
        view = view_of(block, half, k)
        pltpu.make_async_copy(view, view, vis_rsem.at[leg * chunks + k]).wait()

    def sent(k, leg):
        view = view_of(0, 0, k)
        pltpu.make_async_copy(view, view, vis_ssem.at[leg * chunks + k]).wait()

    pair = {"canvas": other}
    diagonal = {"seq": s_diag, "canvas": other}
    placed = matmul(places, came_rows).astype(BF16)
    for k in range(chunks):
        for h in range(2):
            part_rows = placed[h * 128 + k * size:h * 128 + (k + 1) * size, :]
            vis[c, c, k * size:(k + 1) * size, h * QUART:(h + 1) * QUART] = part_rows
        pass_on(c, c, c, k, pair, 0)
    ship(up_v, f_left, 2, mate, 12)
    ship(up_v, f_right, 2, mate, 13)
    for k in range(chunks):
        arrived(other, other, k, 0)
        pass_on(other, other, c, k, diagonal, 1)
    landed(down_v, f_left, 0, 2)
    ship(down_v, f_left, 0, f_right, 8)
    landed(down_v, f_right, 1, 5)
    ship(down_v, f_right, 1, f_left, 9)
    for k in range(chunks):
        arrived(other, c, k, 1)
        pass_on(other, c, other, k, pair, 2)

    qkv_load.wait()

    def project(block):
        rows = pl.ds(pl.multiple_of(block * 128, 128), 128)
        normed[...] = normalised(jnp.concatenate([vis[block, 0], vis[block, 1]], axis=1).astype(F32)).astype(BF16)
        k_s[rows, :] = matmul(normed[...], qkv_v[1]).astype(BF16)
        v_s[rows, :] = matmul(normed[...], qkv_v[2]).astype(BF16)

        @pl.when(block == 0)
        def _():
            q_s[...] = matmul(normed[...], qkv_v[0]).astype(BF16)

    project(other)
    landed(up_v, f_far, 0, 6)
    landed(up_v, f_far, 1, 7)
    ship(up_v, f_far, 2, mate, 16)
    for k in range(chunks):
        arrived(c, other, k, 2)
    project(c)

    low = lax.broadcasted_iota(jnp.int32, (128, 128), 1) < 64
    att_copies = []
    for p in range(4):
        lanes = pl.ds(p * 128, 128)
        q_pair, k_pair, v_pair = q_s[:, lanes], k_s[:, lanes], v_s[:, lanes]
        mixed = []
        for e in range(2):
            q_one = jnp.where(low == (e == 0), q_pair.astype(F32), 0.0).astype(BF16)
            scores = matmul_nt(q_one, k_pair) * 0.125
            expo = jnp.exp(scores - jnp.max(scores, axis=-1, keepdims=True))
            total = jnp.sum(expo, axis=-1, keepdims=True)
            mixed.append(matmul(expo.astype(BF16), v_pair) / total)
        att[c, p] = jnp.where(low, mixed[0], mixed[1]).astype(BF16)
        copy = pltpu.make_async_remote_copy(
            src_ref=att.at[c, p], dst_ref=att.at[c, p], send_sem=att_sem.at[p], recv_sem=att_sem.at[4 + p],
            device_id=pair, device_id_type=MESH,
        )
        copy.start()
        att_copies.append(copy)

    landed(down_v, f_left, 1, 3)
    ship(down_v, f_left, 2, mate, 14)
    landed(down_v, f_right, 0, 4)
    ship(down_v, f_right, 2, mate, 15)

    out_load.wait()

    def mix(half):
        rows = pl.ds(pl.multiple_of(half * HALF, HALF), HALF)
        heads = jnp.concatenate([att[half, p] for p in range(4)], axis=1)
        return matmul(heads, out_v[rows, :])

    visible = jnp.concatenate([vis[0, 0], vis[0, 1]], axis=1).astype(F32)
    resid[...] = visible + mix(c)
    for copy in att_copies:
        copy.wait_recv()
    resid[...] += mix(other)
    normed2[...] = normalised(resid[...]).astype(BF16)

    landed(down_v, f_far, 0, 8)
    landed(down_v, f_far, 1, 9)
    ship(down_v, f_far, 2, mate, 17)

    landed(up_v, mate, 2, 10)
    landed(up_v, m_left, 2, 12)
    landed(up_v, m_right, 2, 13)
    landed(up_v, m_far, 2, 16)

    def widen(n, carry):
        cols = pl.ds(pl.multiple_of(n * 256, 256), 256)
        hidden[:, cols] = gelu(matmul(normed2[...], up_v[:, cols])).astype(BF16)
        return carry

    lax.fori_loop(0, 8, widen, 0)

    here = pl.ds(pl.multiple_of(c * 64, 64), 64)
    there = pl.ds(pl.multiple_of(other * 64, 64), 64)
    chip = f // 2
    y_copies = []
    for n, (step, shard, index_r) in enumerate(((0, mate, 11), (3, m_left, 14), (1, m_right, 15), (2, m_far, 17))):
        landed(down_v, shard, 2, index_r)
        cols = pl.ds(pl.multiple_of(lax.rem(chip + step, 4) * 256, 256), 256)
        part[:, cols] = matmul_nt(hidden[...], down_v[cols, :])
        y_out[n] = part[there, cols].astype(BF16)
        copy = pltpu.make_async_remote_copy(
            src_ref=y_out.at[n], dst_ref=y_in.at[n], send_sem=y_ssem.at[n], recv_sem=y_rsem.at[n],
            device_id=pair, device_id_type=MESH,
        )
        copy.start()
        y_copies.append(copy)
    for n, step in enumerate((0, 3, 1, 2)):
        cols = pl.ds(pl.multiple_of(lax.rem(chip + step, 4) * 256, 256), 256)
        y_copies[n].wait_recv()
        y_ref[:, cols] = (resid[here, cols] + part[here, cols] + y_in[n].astype(F32)).astype(BF16)

    pltpu.make_async_copy(lab_mid.at[three], lab_mid.at[three], a2a_sem.at[0]).wait()
    pltpu.make_async_copy(send.at[three], send.at[three], a2a_sem.at[2]).wait()
    pltpu.make_async_copy(lab_in.at[others], lab_in.at[others], a2a_sem.at[6]).wait()
    pltpu.make_async_copy(recv.at[others], recv.at[others], a2a_sem.at[9]).wait()
    for leg in range(3):
        for k in range(chunks):
            sent(k, leg)
    for copy in shipped:
        copy.wait_send()
    for copy in att_copies + y_copies:
        copy.wait_send()


def shards(chunks, patch_tokens, keep_mask, slot_index, tile_map, qkv_proj, out_proj, up_proj, down_proj):
    n_seq = lax.axis_size("seq")
    freq = jnp.asarray((10000.0 ** (-np.arange(QUART) / QUART)).astype(np.float32)).reshape(1, QUART)
    qkv = jnp.transpose(qkv_proj, (1, 2, 0, 3)).reshape(3, D, HALF)
    hbm = pl.BlockSpec(memory_space=pltpu.HBM)
    vmem = pl.BlockSpec(memory_space=pltpu.VMEM)
    y = pl.pallas_call(
        functools.partial(kernel, n_seq, chunks),
        name="encoder_layer",
        out_shape=pltpu.VMEM((64, D), BF16),
        in_specs=[hbm] * 9,
        out_specs=vmem,
        scratch_shapes=[
            pltpu.SMEM((1, 16), jnp.int32),
            pltpu.VMEM((1, 256), jnp.int32),
            pltpu.VMEM((1, 256), jnp.int32),
            pltpu.VMEM((1, QUART), F32),
            pltpu.VMEM((256, HALF), BF16),
            pltpu.VMEM((3, D, HALF), BF16),
            pltpu.VMEM((D, D), BF16),
            pltpu.VMEM((D, 2048), BF16),
            pltpu.VMEM((D, 2048), BF16),
            pltpu.VMEM((2, 256, QUART), BF16),
            pltpu.VMEM((4, n_seq // 4, 8, QUART), BF16),
            pltpu.VMEM((4, n_seq // 4, 8, QUART), BF16),
            pltpu.VMEM((n_seq // 4, 4, 8, QUART), BF16),
            pltpu.VMEM((1, 128), F32),
            pltpu.VMEM((4, 1, 128), F32),
            pltpu.VMEM((n_seq // 4, 4, 1, 128), F32),
            pltpu.VMEM((2, 2, 128, HALF), BF16),
            pltpu.VMEM((128, D), BF16),
            pltpu.VMEM((128, HALF), BF16),
            pltpu.VMEM((256, HALF), BF16),
            pltpu.VMEM((256, HALF), BF16),
            pltpu.VMEM((2, 4, 128, 128), BF16),
            pltpu.VMEM((128, D), F32),
            pltpu.VMEM((128, D), BF16),
            pltpu.VMEM((128, 2048), BF16),
            pltpu.VMEM((128, D), F32),
            pltpu.VMEM((4, 64, 256), BF16),
            pltpu.VMEM((4, 64, 256), BF16),
            pltpu.SemaphoreType.REGULAR,
            pltpu.SemaphoreType.DMA((9,)),
            pltpu.SemaphoreType.DMA((11,)),
            pltpu.SemaphoreType.DMA((4,)),
            pltpu.SemaphoreType.DMA((3 * chunks,)),
            pltpu.SemaphoreType.DMA((3 * chunks,)),
            pltpu.SemaphoreType.DMA((18,)),
            pltpu.SemaphoreType.DMA((18,)),
            pltpu.SemaphoreType.DMA((8,)),
            pltpu.SemaphoreType.DMA((4,)),
            pltpu.SemaphoreType.DMA((4,)),
        ],
        compiler_params=pltpu.CompilerParams(
            collective_id=0, has_side_effects=True, vmem_limit_bytes=58 * 1024 * 1024
        ),
    )(*[
        pltpu.with_memory_space_constraint(operand, pltpu.HBM)
        for operand in (tile_map, keep_mask, slot_index, freq, patch_tokens, qkv, out_proj, up_proj, down_proj)
    ])
    return y[None]


def solution(mesh):
    placed = (
        P("fsdp", "seq", None),
        P("fsdp", "seq"),
        P("fsdp", "seq"),
        P("fsdp", "seq"),
        P(None, "canvas", None, None),
        P(),
        P("fsdp", "canvas"),
        P("fsdp", "canvas"),
    )
    return jax.shard_map(
        functools.partial(shards, 4),
        mesh=mesh,
        in_specs=placed,
        out_specs=P("fsdp", ("seq", "canvas"), None),
        check_vma=False,
    )
```

```python
import functools

import jax
import jax.numpy as jnp
import numpy as np
from jax import lax
from jax.experimental import pallas as pl
from jax.experimental.pallas import tpu as pltpu
from jax.sharding import PartitionSpec as P

D = 1024
HALF = 512
QUART = 256
EPS = 1e-06
MESH = pl.DeviceIdType.MESH
F32 = jnp.float32
BF16 = jnp.bfloat16


def normalised(values):
    centered = values - jnp.mean(values, axis=-1, keepdims=True)
    spread = jnp.mean(centered * centered, axis=-1, keepdims=True)
    return centered * lax.rsqrt(spread + EPS)


def matmul(left, right):
    return jnp.dot(left, right, preferred_element_type=F32)


def matmul_nt(left, right):
    return lax.dot_general(left, right, (((1,), (1,)), ((), ())), preferred_element_type=F32)


def gelu(x):
    return 0.5 * x * (1.0 + lax.erf(x * (0.5**0.5)))


def kernel(
    n_seq, chunks,
    tile_hbm, keep_hbm, slot_hbm, freq_hbm, patch_hbm, qkv_hbm, out_hbm, up_hbm, down_hbm,
    y_ref,
    tile_ref, keep_ref, slot_ref, freq_ref, patch_v, qkv_v, out_v, up_v, down_v,
    emb, send, mid, recv, lab_out, lab_mid, lab_in, vis, normed, q_s, k_s, v_s, att, resid, normed2, hidden, part, y_out, y_in,
    met_sem, load_sem, a2a_sem, y_sem, vis_ssem, vis_rsem, w_ssem, w_rsem, att_sem, y_ssem, y_rsem,
):
    s = lax.axis_index("seq")
    f = lax.axis_index("fsdp")
    c = lax.axis_index("canvas")
    other = 1 - c
    f_right, f_left, f_far = lax.rem(f + 2, 8), lax.rem(f + 6, 8), lax.rem(f + 4, 8)
    mate = f + 1 - 2 * lax.rem(f, 2)
    m_right, m_left, m_far = lax.rem(mate + 2, 8), lax.rem(mate + 6, 8), lax.rem(mate + 4, 8)
    block_in = lax.rem(s + n_seq - c, n_seq)
    s_diag = lax.rem(s + n_seq + 2 * c - 1, n_seq)

    barrier = pltpu.get_barrier_semaphore()
    n_z = n_seq // 4
    z, y_hi = s // 4, lax.rem(s, 4)

    def peer_at(dz, dy):
        return lax.rem(z + dz + n_z, n_z) * 4 + lax.rem(y_hi + dy, 4)

    def far_first(j, reach):
        return (reach - (j + 1) // 2) * (1 - 2 * lax.rem(j, 2))

    for dy in (2, 1, 3):
        pl.semaphore_signal(barrier, inc=1, device_id={"seq": peer_at(0, dy)}, device_id_type=MESH)

    def greet(j, carry):
        dz = (n_z // 4 - j // 2) * (1 - 2 * lax.rem(j, 2))
        pl.semaphore_signal(barrier, inc=1, device_id={"seq": peer_at(dz, 0)}, device_id_type=MESH)
        return carry

    lax.fori_loop(0, n_z // 2, greet, 0)
    for peer in (f_right, f_left, mate):
        pl.semaphore_signal(barrier, inc=1, device_id={"fsdp": peer}, device_id_type=MESH)
    pl.semaphore_signal(barrier, inc=1, device_id={"canvas": other}, device_id_type=MESH)
    pl.semaphore_signal(barrier, inc=1, device_id={"seq": s_diag, "canvas": other}, device_id_type=MESH)

    col0 = pl.multiple_of(c * HALF, HALF)
    patch_load = pltpu.make_async_copy(patch_hbm.at[0, :, pl.ds(col0, HALF)], patch_v, load_sem.at[0])
    qkv_load = pltpu.make_async_copy(qkv_hbm, qkv_v, load_sem.at[1])
    out_load = pltpu.make_async_copy(out_hbm, out_v, load_sem.at[2])

    def rows_of(shard):
        return pl.ds(pl.multiple_of(shard * 128, 128), 128)

    up_load = pltpu.make_async_copy(up_hbm, up_v.at[rows_of(f)], load_sem.at[3])
    down_load = pltpu.make_async_copy(down_hbm, down_v.at[rows_of(f)], load_sem.at[4])
    index_loads = [
        pltpu.make_async_copy(keep_hbm, keep_ref, load_sem.at[5]),
        pltpu.make_async_copy(slot_hbm, slot_ref, load_sem.at[6]),
        pltpu.make_async_copy(freq_hbm, freq_ref, load_sem.at[7]),
        pltpu.make_async_copy(tile_hbm, tile_ref, load_sem.at[8]),
    ]
    for load in index_loads:
        load.start()
    patch_load.start()

    for load in index_loads:
        load.wait()
    slot = slot_ref[...]
    kept = keep_ref[...] == 1
    target = slot // 128
    lane4 = lax.rem(slot, 4)
    group = lax.rem(slot, 128) // 4
    first = jnp.where(kept & (lane4 == 0), target, -1)
    group_val = jnp.broadcast_to((group + 1).astype(F32), (8, 256)).astype(BF16)
    t_rows = lax.broadcasted_iota(jnp.int32, (128, 256), 0)
    hit = jnp.where(t_rows == first, 1.0, 0.0).astype(BF16)
    labels = matmul_nt(group_val, hit)
    lab_out[...] = labels[0:1, :]

    patch_load.wait()
    for load in (up_load, down_load, qkv_load, out_load):
        load.start()
    freq = freq_ref[...]
    within = lax.broadcasted_iota(jnp.int32, (16, QUART), 0)
    cell = jnp.where(c == 0, within // 4, lax.rem(within, 4))
    two_tiles = lax.broadcasted_iota(jnp.int32, (8, QUART), 0)

    def corner(t):
        tile = tile_ref[0, t]
        return jnp.where(c == 0, tile // 32, lax.rem(tile, 32)) * 4

    def embed(pair_at, carry):
        base = jnp.where(two_tiles < 4, corner(pair_at * 2), corner(pair_at * 2 + 1) - 4)
        angle = (base + two_tiles).astype(F32) * freq
        for quarter, table in enumerate((jnp.sin(angle), jnp.cos(angle))):
            for e in range(2):
                rows = pl.ds(pl.multiple_of(pair_at * 32 + e * 16, 16), 16)
                added = jnp.broadcast_to(table[e * 4:e * 4 + 1, :], (16, QUART))
                for k in range(1, 4):
                    added = jnp.where(cell == k, table[e * 4 + k:e * 4 + k + 1, :], added)
                tokens = patch_v[rows, quarter * QUART:(quarter + 1) * QUART].astype(F32)
                emb[quarter, rows, :] = (tokens + added).astype(BF16)
        return carry

    lax.fori_loop(0, 8, embed, 0)

    key = jnp.where(kept, target * 4 + lane4, -1000)
    row_i = lax.broadcasted_iota(jnp.int32, (512, QUART), 0)
    slot_i = row_i // 8
    block_i = lax.rem(lax.rem(slot_i, n_z) * 4 + slot_i // n_z + n_seq - c, n_seq)
    row_key = block_i * 4 + lax.rem(row_i, 4) + lax.rem(row_i // 4, 2) * 256
    pick0 = jnp.where(row_key == key, 1.0, 0.0).astype(BF16)
    pick1 = jnp.where(row_key == key + 256, 1.0, 0.0).astype(BF16)
    packed = matmul(pick0, emb[0]) + matmul(pick1, emb[1])
    send[...] = packed.astype(BF16).reshape(4, n_z, 8, QUART)

    pl.semaphore_wait(barrier, n_z // 2 + 8)
    for dz in (n_z // 4, -(n_z // 4)):
        pl.semaphore_signal(met_sem, inc=1, device_id={"seq": peer_at(dz, 0)}, device_id_type=MESH)

    own_label = pltpu.make_async_copy(lab_out, lab_mid.at[y_hi], a2a_sem.at[4])
    own_label.start()
    own_rows = pltpu.make_async_copy(send.at[y_hi], mid.at[y_hi], a2a_sem.at[5])
    own_rows.start()
    for dy in (2, 1, 3):
        pltpu.make_async_remote_copy(
            src_ref=lab_out, dst_ref=lab_mid.at[y_hi], send_sem=a2a_sem.at[0], recv_sem=a2a_sem.at[1],
            device_id={"seq": peer_at(0, dy)}, device_id_type=MESH,
        ).start()
    n_part = n_z // 4
    parts = [lax.rem(z // n_part + off, 4) for off in (2, 3, 1, 0)]
    for q in parts:
        column = pl.ds(q * n_part, n_part)
        for dy in (2, 1, 3):
            pltpu.make_async_remote_copy(
                src_ref=send.at[lax.rem(y_hi + dy, 4), column], dst_ref=mid.at[y_hi, column],
                send_sem=a2a_sem.at[2], recv_sem=y_sem.at[q],
                device_id={"seq": peer_at(0, dy)}, device_id_type=MESH,
            ).start()

    def piece(buf, shard, part):
        first_row, count = ((0, 64), (64, 64), (0, 128))[part]
        return buf.at[pl.ds(pl.multiple_of(shard * 128 + first_row, 64), count)]

    shipped = []

    def ship(buf, shard, part, to, index_r):
        copy = pltpu.make_async_remote_copy(
            src_ref=piece(buf, shard, part), dst_ref=piece(buf, shard, part),
            send_sem=w_ssem.at[len(shipped)], recv_sem=w_rsem.at[index_r],
            device_id={"fsdp": to}, device_id_type=MESH,
        )
        copy.start()
        shipped.append(copy)

    def landed(buf, shard, part, index_r):
        view = piece(buf, shard, part)
        pltpu.make_async_copy(view, view, w_rsem.at[index_r]).wait()

    up_load.wait()
    ship(up_v, f, 2, f_right, 0)
    ship(up_v, f, 2, f_left, 1)
    ship(up_v, f, 2, mate, 10)
    down_load.wait()
    ship(down_v, f, 0, f_right, 2)
    ship(down_v, f, 1, f_left, 5)
    ship(down_v, f, 2, mate, 11)

    pl.semaphore_wait(met_sem, 2)
    own_label.wait()
    three = pl.ds(0, 3)
    pltpu.make_async_copy(lab_mid.at[three], lab_mid.at[three], a2a_sem.at[1]).wait()
    own_labels = pltpu.make_async_copy(lab_mid, lab_in.at[z], a2a_sem.at[8])
    own_labels.start()

    def push_labels(j, carry):
        pltpu.make_async_remote_copy(
            src_ref=lab_mid, dst_ref=lab_in.at[z], send_sem=a2a_sem.at[6], recv_sem=a2a_sem.at[7],
            device_id={"seq": peer_at(far_first(j, n_z // 2), 0)}, device_id_type=MESH,
        ).start()
        return carry

    lax.fori_loop(0, n_z - 1, push_labels, 0)
    own_rows.wait()
    for q in parts:
        came = mid.at[three, pl.ds(q * n_part, n_part)]
        pltpu.make_async_copy(came, came, y_sem.at[q]).wait()
        for j in range(n_part):
            to = q * n_part + j

            @pl.when(to != z)
            def _():
                pltpu.make_async_remote_copy(
                    src_ref=mid.at[:, to], dst_ref=recv.at[z], send_sem=a2a_sem.at[9], recv_sem=a2a_sem.at[3],
                    device_id={"seq": to * 4 + y_hi}, device_id_type=MESH,
                ).start()

    own_column = pltpu.make_async_copy(mid.at[:, z], recv.at[z], a2a_sem.at[10])
    own_column.start()

    others = pl.ds(0, n_z - 1)
    own_labels.wait()
    pltpu.make_async_copy(lab_in.at[others], lab_in.at[others], a2a_sem.at[7]).wait()
    lane_of = lax.broadcasted_iota(jnp.int32, (8, 128), 1)
    mine = jnp.where(lane_of == block_in, 1.0, 0.0).astype(BF16)
    came = matmul_nt(mine, lab_in[...].reshape(n_seq, 128).astype(BF16))
    spread_r = lax.broadcasted_iota(jnp.int32, (n_seq, 512), 0)
    spread_c = lax.broadcasted_iota(jnp.int32, (n_seq, 512), 1)
    spread = jnp.where(spread_r == spread_c // 8, 1.0, 0.0).astype(BF16)
    label_of = matmul(came.astype(BF16), spread).astype(jnp.int32)
    col_i = lax.broadcasted_iota(jnp.int32, (8, 512), 1)
    row_of = label_of * 4 - 4 + lax.rem(col_i, 4)
    half_of = lax.rem(col_i // 4, 2)
    r_i = lax.broadcasted_iota(jnp.int32, (128, 512), 0)
    places = []
    for h in range(2):
        row_h = jnp.where(half_of == h, row_of, -1)[0:1, :]
        places.append(jnp.where(r_i == row_h, 1.0, 0.0).astype(BF16))
    places = jnp.concatenate(places, axis=0)
    landed(up_v, f_left, 2, 0)
    ship(up_v, f_left, 0, f_right, 6)
    landed(up_v, f_right, 2, 1)
    ship(up_v, f_right, 1, f_left, 7)
    ship(down_v, f, 1, f_right, 3)
    ship(down_v, f, 0, f_left, 4)

    own_column.wait()
    pltpu.make_async_copy(recv.at[others], recv.at[others], a2a_sem.at[3]).wait()
    came_rows = recv[...].reshape(512, QUART)
    size = 128 // chunks

    def view_of(block, half, k):
        return vis.at[block, half, pl.ds(k * size, size), :]

    def pass_on(block, half, to_block, k, to, leg):
        pltpu.make_async_remote_copy(
            src_ref=view_of(block, half, k), dst_ref=view_of(to_block, half, k),
            send_sem=vis_ssem.at[leg * chunks + k], recv_sem=vis_rsem.at[leg * chunks + k],
            device_id=to, device_id_type=MESH,
        ).start()

    def arrived(block, half, k, leg):
        view = view_of(block, half, k)
        pltpu.make_async_copy(view, view, vis_rsem.at[leg * chunks + k]).wait()

    def sent(k, leg):
        view = view_of(0, 0, k)
        pltpu.make_async_copy(view, view, vis_ssem.at[leg * chunks + k]).wait()

    pair = {"canvas": other}
    diagonal = {"seq": s_diag, "canvas": other}
    placed = matmul(places, came_rows).astype(BF16)
    for k in range(chunks):
        for h in range(2):
            part_rows = placed[h * 128 + k * size:h * 128 + (k + 1) * size, :]
            vis[c, c, k * size:(k + 1) * size, h * QUART:(h + 1) * QUART] = part_rows
        pass_on(c, c, c, k, pair, 0)
    ship(up_v, f_left, 2, mate, 12)
    ship(up_v, f_right, 2, mate, 13)
    for k in range(chunks):
        arrived(other, other, k, 0)
        pass_on(other, other, c, k, diagonal, 1)
    for k in range(chunks):
        arrived(other, c, k, 1)
        pass_on(other, c, other, k, pair, 2)

    landed(down_v, f_left, 0, 2)
    ship(down_v, f_left, 0, f_right, 8)
    landed(down_v, f_right, 1, 5)
    ship(down_v, f_right, 1, f_left, 9)
    qkv_load.wait()

    def project(block):
        rows = pl.ds(pl.multiple_of(block * 128, 128), 128)
        normed[...] = normalised(jnp.concatenate([vis[block, 0], vis[block, 1]], axis=1).astype(F32)).astype(BF16)
        k_s[rows, :] = matmul(normed[...], qkv_v[1]).astype(BF16)
        v_s[rows, :] = matmul(normed[...], qkv_v[2]).astype(BF16)

        @pl.when(block == 0)
        def _():
            q_s[...] = matmul(normed[...], qkv_v[0]).astype(BF16)

    project(other)
    landed(up_v, f_far, 0, 6)
    landed(up_v, f_far, 1, 7)
    ship(up_v, f_far, 2, mate, 16)
    for k in range(chunks):
        arrived(c, other, k, 2)
    project(c)

    low = lax.broadcasted_iota(jnp.int32, (128, 128), 1) < 64
    att_copies = []
    for p in range(4):
        lanes = pl.ds(p * 128, 128)
        q_pair, k_pair, v_pair = q_s[:, lanes], k_s[:, lanes], v_s[:, lanes]
        mixed = []
        for e in range(2):
            q_one = jnp.where(low == (e == 0), q_pair.astype(F32), 0.0).astype(BF16)
            scores = matmul_nt(q_one, k_pair) * 0.125
            expo = jnp.exp(scores - jnp.max(scores, axis=-1, keepdims=True))
            total = jnp.sum(expo, axis=-1, keepdims=True)
            mixed.append(matmul(expo.astype(BF16), v_pair) / total)
        att[c, p] = jnp.where(low, mixed[0], mixed[1]).astype(BF16)
        copy = pltpu.make_async_remote_copy(
            src_ref=att.at[c, p], dst_ref=att.at[c, p], send_sem=att_sem.at[p], recv_sem=att_sem.at[4 + p],
            device_id=pair, device_id_type=MESH,
        )
        copy.start()
        att_copies.append(copy)

    landed(down_v, f_left, 1, 3)
    ship(down_v, f_left, 2, mate, 14)
    landed(down_v, f_right, 0, 4)
    ship(down_v, f_right, 2, mate, 15)

    out_load.wait()

    def mix(half):
        rows = pl.ds(pl.multiple_of(half * HALF, HALF), HALF)
        heads = jnp.concatenate([att[half, p] for p in range(4)], axis=1)
        return matmul(heads, out_v[rows, :])

    visible = jnp.concatenate([vis[0, 0], vis[0, 1]], axis=1).astype(F32)
    resid[...] = visible + mix(c)
    for copy in att_copies:
        copy.wait_recv()
    resid[...] += mix(other)
    normed2[...] = normalised(resid[...]).astype(BF16)

    landed(down_v, f_far, 0, 8)
    landed(down_v, f_far, 1, 9)
    ship(down_v, f_far, 2, mate, 17)

    landed(up_v, mate, 2, 10)
    landed(up_v, m_left, 2, 12)
    landed(up_v, m_right, 2, 13)
    landed(up_v, m_far, 2, 16)

    def widen(n, carry):
        cols = pl.ds(pl.multiple_of(n * 256, 256), 256)
        hidden[:, cols] = gelu(matmul(normed2[...], up_v[:, cols])).astype(BF16)
        return carry

    lax.fori_loop(0, 8, widen, 0)

    here = pl.ds(pl.multiple_of(c * 64, 64), 64)
    there = pl.ds(pl.multiple_of(other * 64, 64), 64)
    chip = f // 2
    y_copies = []
    for n, (step, shard, index_r) in enumerate(((0, mate, 11), (3, m_left, 14), (1, m_right, 15), (2, m_far, 17))):
        landed(down_v, shard, 2, index_r)
        cols = pl.ds(pl.multiple_of(lax.rem(chip + step, 4) * 256, 256), 256)
        part[:, cols] = matmul_nt(hidden[...], down_v[cols, :])
        y_out[n] = part[there, cols].astype(BF16)
        copy = pltpu.make_async_remote_copy(
            src_ref=y_out.at[n], dst_ref=y_in.at[n], send_sem=y_ssem.at[n], recv_sem=y_rsem.at[n],
            device_id=pair, device_id_type=MESH,
        )
        copy.start()
        y_copies.append(copy)
    for n, step in enumerate((0, 3, 1, 2)):
        cols = pl.ds(pl.multiple_of(lax.rem(chip + step, 4) * 256, 256), 256)
        y_copies[n].wait_recv()
        y_ref[:, cols] = (resid[here, cols] + part[here, cols] + y_in[n].astype(F32)).astype(BF16)

    pltpu.make_async_copy(lab_mid.at[three], lab_mid.at[three], a2a_sem.at[0]).wait()
    pltpu.make_async_copy(send.at[three], send.at[three], a2a_sem.at[2]).wait()
    pltpu.make_async_copy(lab_in.at[others], lab_in.at[others], a2a_sem.at[6]).wait()
    pltpu.make_async_copy(recv.at[others], recv.at[others], a2a_sem.at[9]).wait()
    for leg in range(3):
        for k in range(chunks):
            sent(k, leg)
    for copy in shipped:
        copy.wait_send()
    for copy in att_copies + y_copies:
        copy.wait_send()


def shards(chunks, patch_tokens, keep_mask, slot_index, tile_map, qkv_proj, out_proj, up_proj, down_proj):
    n_seq = lax.axis_size("seq")
    freq = jnp.asarray((10000.0 ** (-np.arange(QUART) / QUART)).astype(np.float32)).reshape(1, QUART)
    qkv = jnp.transpose(qkv_proj, (1, 2, 0, 3)).reshape(3, D, HALF)
    hbm = pl.BlockSpec(memory_space=pltpu.HBM)
    vmem = pl.BlockSpec(memory_space=pltpu.VMEM)
    y = pl.pallas_call(
        functools.partial(kernel, n_seq, chunks),
        name="encoder_layer",
        out_shape=pltpu.VMEM((64, D), BF16),
        in_specs=[hbm] * 9,
        out_specs=vmem,
        scratch_shapes=[
            pltpu.SMEM((1, 16), jnp.int32),
            pltpu.VMEM((1, 256), jnp.int32),
            pltpu.VMEM((1, 256), jnp.int32),
            pltpu.VMEM((1, QUART), F32),
            pltpu.VMEM((256, HALF), BF16),
            pltpu.VMEM((3, D, HALF), BF16),
            pltpu.VMEM((D, D), BF16),
            pltpu.VMEM((D, 2048), BF16),
            pltpu.VMEM((D, 2048), BF16),
            pltpu.VMEM((2, 256, QUART), BF16),
            pltpu.VMEM((4, n_seq // 4, 8, QUART), BF16),
            pltpu.VMEM((4, n_seq // 4, 8, QUART), BF16),
            pltpu.VMEM((n_seq // 4, 4, 8, QUART), BF16),
            pltpu.VMEM((1, 128), F32),
            pltpu.VMEM((4, 1, 128), F32),
            pltpu.VMEM((n_seq // 4, 4, 1, 128), F32),
            pltpu.VMEM((2, 2, 128, HALF), BF16),
            pltpu.VMEM((128, D), BF16),
            pltpu.VMEM((128, HALF), BF16),
            pltpu.VMEM((256, HALF), BF16),
            pltpu.VMEM((256, HALF), BF16),
            pltpu.VMEM((2, 4, 128, 128), BF16),
            pltpu.VMEM((128, D), F32),
            pltpu.VMEM((128, D), BF16),
            pltpu.VMEM((128, 2048), BF16),
            pltpu.VMEM((128, D), F32),
            pltpu.VMEM((4, 64, 256), BF16),
            pltpu.VMEM((4, 64, 256), BF16),
            pltpu.SemaphoreType.REGULAR,
            pltpu.SemaphoreType.DMA((9,)),
            pltpu.SemaphoreType.DMA((11,)),
            pltpu.SemaphoreType.DMA((4,)),
            pltpu.SemaphoreType.DMA((3 * chunks,)),
            pltpu.SemaphoreType.DMA((3 * chunks,)),
            pltpu.SemaphoreType.DMA((18,)),
            pltpu.SemaphoreType.DMA((18,)),
            pltpu.SemaphoreType.DMA((8,)),
            pltpu.SemaphoreType.DMA((4,)),
            pltpu.SemaphoreType.DMA((4,)),
        ],
        compiler_params=pltpu.CompilerParams(
            collective_id=0, has_side_effects=True, vmem_limit_bytes=58 * 1024 * 1024
        ),
    )(*[
        pltpu.with_memory_space_constraint(operand, pltpu.HBM)
        for operand in (tile_map, keep_mask, slot_index, freq, patch_tokens, qkv, out_proj, up_proj, down_proj)
    ])
    return y[None]


def solution(mesh):
    placed = (
        P("fsdp", "seq", None),
        P("fsdp", "seq"),
        P("fsdp", "seq"),
        P("fsdp", "seq"),
        P(None, "canvas", None, None),
        P(),
        P("fsdp", "canvas"),
        P("fsdp", "canvas"),
    )
    return jax.shard_map(
        functools.partial(shards, 4),
        mesh=mesh,
        in_specs=placed,
        out_specs=P("fsdp", ("seq", "canvas"), None),
        check_vma=False,
    )
```

```python
import functools

import jax
import jax.numpy as jnp
import numpy as np
from jax import lax
from jax.experimental import pallas as pl
from jax.experimental.pallas import tpu as pltpu
from jax.sharding import PartitionSpec as P

D = 1024
HALF = 512
QUART = 256
EPS = 1e-06
MESH = pl.DeviceIdType.MESH
F32 = jnp.float32
BF16 = jnp.bfloat16


def normalised(values):
    centered = values - jnp.mean(values, axis=-1, keepdims=True)
    spread = jnp.mean(centered * centered, axis=-1, keepdims=True)
    return centered * lax.rsqrt(spread + EPS)


def matmul(left, right):
    return jnp.dot(left, right, preferred_element_type=F32)


def matmul_nt(left, right):
    return lax.dot_general(left, right, (((1,), (1,)), ((), ())), preferred_element_type=F32)


def gelu(x):
    return 0.5 * x * (1.0 + lax.erf(x * (0.5**0.5)))


def kernel(
    n_seq, chunks,
    tile_hbm, keep_hbm, slot_hbm, freq_hbm, patch_hbm, qkv_hbm, out_hbm, up_hbm, down_hbm,
    y_ref,
    tile_ref, keep_ref, slot_ref, freq_ref, patch_v, qkv_v, out_v, up_v, down_v,
    emb, send, mid, recv, lab_out, lab_mid, lab_in, vis, normed, q_s, k_s, v_s, att, resid, normed2, hidden, part, y_out, y_in,
    met_sem, load_sem, a2a_sem, y_sem, vis_ssem, vis_rsem, w_ssem, w_rsem, att_sem, y_ssem, y_rsem,
):
    s = lax.axis_index("seq")
    f = lax.axis_index("fsdp")
    c = lax.axis_index("canvas")
    other = 1 - c
    f_right, f_left, f_far = lax.rem(f + 2, 8), lax.rem(f + 6, 8), lax.rem(f + 4, 8)
    mate = f + 1 - 2 * lax.rem(f, 2)
    m_right, m_left, m_far = lax.rem(mate + 2, 8), lax.rem(mate + 6, 8), lax.rem(mate + 4, 8)
    block_in = lax.rem(s + n_seq - c, n_seq)
    s_diag = lax.rem(s + n_seq + 2 * c - 1, n_seq)

    col0 = pl.multiple_of(c * HALF, HALF)
    patch_load = pltpu.make_async_copy(patch_hbm.at[0, :, pl.ds(col0, HALF)], patch_v, load_sem.at[0])
    qkv_load = pltpu.make_async_copy(qkv_hbm, qkv_v, load_sem.at[1])
    out_load = pltpu.make_async_copy(out_hbm, out_v, load_sem.at[2])

    def rows_of(shard):
        return pl.ds(pl.multiple_of(shard * 128, 128), 128)

    up_load = pltpu.make_async_copy(up_hbm, up_v.at[rows_of(f)], load_sem.at[3])
    down_load = pltpu.make_async_copy(down_hbm, down_v.at[rows_of(f)], load_sem.at[4])
    index_loads = [
        pltpu.make_async_copy(keep_hbm, keep_ref, load_sem.at[5]),
        pltpu.make_async_copy(slot_hbm, slot_ref, load_sem.at[6]),
        pltpu.make_async_copy(freq_hbm, freq_ref, load_sem.at[7]),
        pltpu.make_async_copy(tile_hbm, tile_ref, load_sem.at[8]),
    ]
    for load in index_loads:
        load.start()
    patch_load.start()

    barrier = pltpu.get_barrier_semaphore()
    n_z = n_seq // 4
    z, y_hi = s // 4, lax.rem(s, 4)

    def peer_at(dz, dy):
        return lax.rem(z + dz + n_z, n_z) * 4 + lax.rem(y_hi + dy, 4)

    def far_first(j, reach):
        return (reach - (j + 1) // 2) * (1 - 2 * lax.rem(j, 2))

    for dy in (2, 1, 3):
        pl.semaphore_signal(barrier, inc=1, device_id={"seq": peer_at(0, dy)}, device_id_type=MESH)

    def greet(j, carry):
        dz = (n_z // 4 - j // 2) * (1 - 2 * lax.rem(j, 2))
        pl.semaphore_signal(barrier, inc=1, device_id={"seq": peer_at(dz, 0)}, device_id_type=MESH)
        return carry

    lax.fori_loop(0, n_z // 2, greet, 0)
    for peer in (f_right, f_left, mate):
        pl.semaphore_signal(barrier, inc=1, device_id={"fsdp": peer}, device_id_type=MESH)
    pl.semaphore_signal(barrier, inc=1, device_id={"canvas": other}, device_id_type=MESH)
    pl.semaphore_signal(barrier, inc=1, device_id={"seq": s_diag, "canvas": other}, device_id_type=MESH)

    for load in index_loads:
        load.wait()
    slot = slot_ref[...]
    kept = keep_ref[...] == 1
    target = slot // 128
    lane4 = lax.rem(slot, 4)
    group = lax.rem(slot, 128) // 4
    first = jnp.where(kept & (lane4 == 0), target, -1)
    group_val = jnp.broadcast_to((group + 1).astype(F32), (8, 256)).astype(BF16)
    t_rows = lax.broadcasted_iota(jnp.int32, (128, 256), 0)
    hit = jnp.where(t_rows == first, 1.0, 0.0).astype(BF16)
    labels = matmul_nt(group_val, hit)
    lab_out[...] = labels[0:1, :]

    patch_load.wait()
    for load in (up_load, down_load, qkv_load, out_load):
        load.start()
    freq = freq_ref[...]
    within = lax.broadcasted_iota(jnp.int32, (16, QUART), 0)
    cell = jnp.where(c == 0, within // 4, lax.rem(within, 4))
    two_tiles = lax.broadcasted_iota(jnp.int32, (8, QUART), 0)

    def corner(t):
        tile = tile_ref[0, t]
        return jnp.where(c == 0, tile // 32, lax.rem(tile, 32)) * 4

    def embed(pair_at, carry):
        base = jnp.where(two_tiles < 4, corner(pair_at * 2), corner(pair_at * 2 + 1) - 4)
        angle = (base + two_tiles).astype(F32) * freq
        for quarter, table in enumerate((jnp.sin(angle), jnp.cos(angle))):
            for e in range(2):
                rows = pl.ds(pl.multiple_of(pair_at * 32 + e * 16, 16), 16)
                added = jnp.broadcast_to(table[e * 4:e * 4 + 1, :], (16, QUART))
                for k in range(1, 4):
                    added = jnp.where(cell == k, table[e * 4 + k:e * 4 + k + 1, :], added)
                tokens = patch_v[rows, quarter * QUART:(quarter + 1) * QUART].astype(F32)
                emb[quarter, rows, :] = (tokens + added).astype(BF16)
        return carry

    lax.fori_loop(0, 8, embed, 0, unroll=4)

    key = jnp.where(kept, target * 4 + lane4, -1000)
    row_i = lax.broadcasted_iota(jnp.int32, (512, QUART), 0)
    slot_i = row_i // 8
    block_i = lax.rem(lax.rem(slot_i, n_z) * 4 + slot_i // n_z + n_seq - c, n_seq)
    row_key = block_i * 4 + lax.rem(row_i, 4) + lax.rem(row_i // 4, 2) * 256
    pick0 = jnp.where(row_key == key, 1.0, 0.0).astype(BF16)
    pick1 = jnp.where(row_key == key + 256, 1.0, 0.0).astype(BF16)
    packed = matmul(pick0, emb[0]) + matmul(pick1, emb[1])
    send[...] = packed.astype(BF16).reshape(4, n_z, 8, QUART)

    pl.semaphore_wait(barrier, n_z // 2 + 8)
    for dz in (n_z // 4, -(n_z // 4)):
        pl.semaphore_signal(met_sem, inc=1, device_id={"seq": peer_at(dz, 0)}, device_id_type=MESH)

    own_label = pltpu.make_async_copy(lab_out, lab_mid.at[y_hi], a2a_sem.at[4])
    own_label.start()
    own_rows = pltpu.make_async_copy(send.at[y_hi], mid.at[y_hi], a2a_sem.at[5])
    own_rows.start()
    for dy in (2, 1, 3):
        pltpu.make_async_remote_copy(
            src_ref=lab_out, dst_ref=lab_mid.at[y_hi], send_sem=a2a_sem.at[0], recv_sem=a2a_sem.at[1],
            device_id={"seq": peer_at(0, dy)}, device_id_type=MESH,
        ).start()
    n_part = n_z // 4
    parts = [lax.rem(z // n_part + off, 4) for off in (2, 3, 1, 0)]
    for q in parts:
        column = pl.ds(q * n_part, n_part)
        for dy in (2, 1, 3):
            pltpu.make_async_remote_copy(
                src_ref=send.at[lax.rem(y_hi + dy, 4), column], dst_ref=mid.at[y_hi, column],
                send_sem=a2a_sem.at[2], recv_sem=y_sem.at[q],
                device_id={"seq": peer_at(0, dy)}, device_id_type=MESH,
            ).start()

    def piece(buf, shard, part):
        first_row, count = ((0, 64), (64, 64), (0, 128))[part]
        return buf.at[pl.ds(pl.multiple_of(shard * 128 + first_row, 64), count)]

    shipped = []

    def ship(buf, shard, part, to, index_r):
        copy = pltpu.make_async_remote_copy(
            src_ref=piece(buf, shard, part), dst_ref=piece(buf, shard, part),
            send_sem=w_ssem.at[len(shipped)], recv_sem=w_rsem.at[index_r],
            device_id={"fsdp": to}, device_id_type=MESH,
        )
        copy.start()
        shipped.append(copy)

    def landed(buf, shard, part, index_r):
        view = piece(buf, shard, part)
        pltpu.make_async_copy(view, view, w_rsem.at[index_r]).wait()

    up_load.wait()
    ship(up_v, f, 2, f_right, 0)
    ship(up_v, f, 2, f_left, 1)
    ship(up_v, f, 2, mate, 10)
    down_load.wait()
    ship(down_v, f, 0, f_right, 2)
    ship(down_v, f, 1, f_left, 5)
    ship(down_v, f, 2, mate, 11)

    pl.semaphore_wait(met_sem, 2)
    own_label.wait()
    three = pl.ds(0, 3)
    pltpu.make_async_copy(lab_mid.at[three], lab_mid.at[three], a2a_sem.at[1]).wait()
    own_labels = pltpu.make_async_copy(lab_mid, lab_in.at[z], a2a_sem.at[8])
    own_labels.start()

    def push_labels(j, carry):
        pltpu.make_async_remote_copy(
            src_ref=lab_mid, dst_ref=lab_in.at[z], send_sem=a2a_sem.at[6], recv_sem=a2a_sem.at[7],
            device_id={"seq": peer_at(far_first(j, n_z // 2), 0)}, device_id_type=MESH,
        ).start()
        return carry

    lax.fori_loop(0, n_z - 1, push_labels, 0)
    own_rows.wait()
    for q in parts:
        came = mid.at[three, pl.ds(q * n_part, n_part)]
        pltpu.make_async_copy(came, came, y_sem.at[q]).wait()
        for j in range(n_part):
            to = q * n_part + j

            @pl.when(to != z)
            def _():
                pltpu.make_async_remote_copy(
                    src_ref=mid.at[:, to], dst_ref=recv.at[z], send_sem=a2a_sem.at[9], recv_sem=a2a_sem.at[3],
                    device_id={"seq": to * 4 + y_hi}, device_id_type=MESH,
                ).start()

    own_column = pltpu.make_async_copy(mid.at[:, z], recv.at[z], a2a_sem.at[10])
    own_column.start()

    others = pl.ds(0, n_z - 1)
    own_labels.wait()
    pltpu.make_async_copy(lab_in.at[others], lab_in.at[others], a2a_sem.at[7]).wait()
    lane_of = lax.broadcasted_iota(jnp.int32, (8, 128), 1)
    mine = jnp.where(lane_of == block_in, 1.0, 0.0).astype(BF16)
    came = matmul_nt(mine, lab_in[...].reshape(n_seq, 128).astype(BF16))
    spread_r = lax.broadcasted_iota(jnp.int32, (n_seq, 512), 0)
    spread_c = lax.broadcasted_iota(jnp.int32, (n_seq, 512), 1)
    spread = jnp.where(spread_r == spread_c // 8, 1.0, 0.0).astype(BF16)
    label_of = matmul(came.astype(BF16), spread).astype(jnp.int32)
    col_i = lax.broadcasted_iota(jnp.int32, (8, 512), 1)
    row_of = label_of * 4 - 4 + lax.rem(col_i, 4)
    half_of = lax.rem(col_i // 4, 2)
    r_i = lax.broadcasted_iota(jnp.int32, (128, 512), 0)
    places = []
    for h in range(2):
        row_h = jnp.where(half_of == h, row_of, -1)[0:1, :]
        places.append(jnp.where(r_i == row_h, 1.0, 0.0).astype(BF16))
    places = jnp.concatenate(places, axis=0)
    landed(up_v, f_left, 2, 0)
    ship(up_v, f_left, 0, f_right, 6)
    landed(up_v, f_right, 2, 1)
    ship(up_v, f_right, 1, f_left, 7)
    ship(down_v, f, 1, f_right, 3)
    ship(down_v, f, 0, f_left, 4)

    own_column.wait()
    pltpu.make_async_copy(recv.at[others], recv.at[others], a2a_sem.at[3]).wait()
    came_rows = recv[...].reshape(512, QUART)
    size = 128 // chunks

    def view_of(block, half, k):
        return vis.at[block, half, pl.ds(k * size, size), :]

    def pass_on(block, half, to_block, k, to, leg):
        pltpu.make_async_remote_copy(
            src_ref=view_of(block, half, k), dst_ref=view_of(to_block, half, k),
            send_sem=vis_ssem.at[leg * chunks + k], recv_sem=vis_rsem.at[leg * chunks + k],
            device_id=to, device_id_type=MESH,
        ).start()

    def arrived(block, half, k, leg):
        view = view_of(block, half, k)
        pltpu.make_async_copy(view, view, vis_rsem.at[leg * chunks + k]).wait()

    def sent(k, leg):
        view = view_of(0, 0, k)
        pltpu.make_async_copy(view, view, vis_ssem.at[leg * chunks + k]).wait()

    pair = {"canvas": other}
    diagonal = {"seq": s_diag, "canvas": other}
    placed = matmul(places, came_rows).astype(BF16)
    for k in range(chunks):
        for h in range(2):
            part_rows = placed[h * 128 + k * size:h * 128 + (k + 1) * size, :]
            vis[c, c, k * size:(k + 1) * size, h * QUART:(h + 1) * QUART] = part_rows
        pass_on(c, c, c, k, pair, 0)
    ship(up_v, f_left, 2, mate, 12)
    ship(up_v, f_right, 2, mate, 13)
    for k in range(chunks):
        arrived(other, other, k, 0)
        pass_on(other, other, c, k, diagonal, 1)
    for k in range(chunks):
        arrived(other, c, k, 1)
        pass_on(other, c, other, k, pair, 2)

    landed(down_v, f_left, 0, 2)
    ship(down_v, f_left, 0, f_right, 8)
    landed(down_v, f_right, 1, 5)
    ship(down_v, f_right, 1, f_left, 9)
    qkv_load.wait()

    def project(block):
        rows = pl.ds(pl.multiple_of(block * 128, 128), 128)
        normed[...] = normalised(jnp.concatenate([vis[block, 0], vis[block, 1]], axis=1).astype(F32)).astype(BF16)
        k_s[rows, :] = matmul(normed[...], qkv_v[1]).astype(BF16)
        v_s[rows, :] = matmul(normed[...], qkv_v[2]).astype(BF16)

        @pl.when(block == 0)
        def _():
            q_s[...] = matmul(normed[...], qkv_v[0]).astype(BF16)

    project(other)
    landed(up_v, f_far, 0, 6)
    landed(up_v, f_far, 1, 7)
    ship(up_v, f_far, 2, mate, 16)
    for k in range(chunks):
        arrived(c, other, k, 2)
    project(c)

    low = lax.broadcasted_iota(jnp.int32, (128, 128), 1) < 64
    att_copies = []
    for p in range(4):
        lanes = pl.ds(p * 128, 128)
        q_pair, k_pair, v_pair = q_s[:, lanes], k_s[:, lanes], v_s[:, lanes]
        mixed = []
        for e in range(2):
            q_one = jnp.where(low == (e == 0), q_pair.astype(F32), 0.0).astype(BF16)
            scores = matmul_nt(q_one, k_pair) * 0.125
            expo = jnp.exp(scores - jnp.max(scores, axis=-1, keepdims=True))
            total = jnp.sum(expo, axis=-1, keepdims=True)
            mixed.append(matmul(expo.astype(BF16), v_pair) / total)
        att[c, p] = jnp.where(low, mixed[0], mixed[1]).astype(BF16)
        copy = pltpu.make_async_remote_copy(
            src_ref=att.at[c, p], dst_ref=att.at[c, p], send_sem=att_sem.at[p], recv_sem=att_sem.at[4 + p],
            device_id=pair, device_id_type=MESH,
        )
        copy.start()
        att_copies.append(copy)

    landed(down_v, f_left, 1, 3)
    ship(down_v, f_left, 2, mate, 14)
    landed(down_v, f_right, 0, 4)
    ship(down_v, f_right, 2, mate, 15)

    out_load.wait()

    def mix(half):
        rows = pl.ds(pl.multiple_of(half * HALF, HALF), HALF)
        heads = jnp.concatenate([att[half, p] for p in range(4)], axis=1)
        return matmul(heads, out_v[rows, :])

    visible = jnp.concatenate([vis[0, 0], vis[0, 1]], axis=1).astype(F32)
    resid[...] = visible + mix(c)
    for copy in att_copies:
        copy.wait_recv()
    resid[...] += mix(other)
    normed2[...] = normalised(resid[...]).astype(BF16)

    landed(down_v, f_far, 0, 8)
    landed(down_v, f_far, 1, 9)
    ship(down_v, f_far, 2, mate, 17)

    landed(up_v, mate, 2, 10)
    landed(up_v, m_left, 2, 12)
    landed(up_v, m_right, 2, 13)
    landed(up_v, m_far, 2, 16)

    def widen(n, carry):
        cols = pl.ds(pl.multiple_of(n * 256, 256), 256)
        hidden[:, cols] = gelu(matmul(normed2[...], up_v[:, cols])).astype(BF16)
        return carry

    lax.fori_loop(0, 8, widen, 0)

    here = pl.ds(pl.multiple_of(c * 64, 64), 64)
    there = pl.ds(pl.multiple_of(other * 64, 64), 64)
    chip = f // 2
    y_copies = []
    for n, (step, shard, index_r) in enumerate(((0, mate, 11), (3, m_left, 14), (1, m_right, 15), (2, m_far, 17))):
        landed(down_v, shard, 2, index_r)
        cols = pl.ds(pl.multiple_of(lax.rem(chip + step, 4) * 256, 256), 256)
        part[:, cols] = matmul_nt(hidden[...], down_v[cols, :])
        y_out[n] = part[there, cols].astype(BF16)
        copy = pltpu.make_async_remote_copy(
            src_ref=y_out.at[n], dst_ref=y_in.at[n], send_sem=y_ssem.at[n], recv_sem=y_rsem.at[n],
            device_id=pair, device_id_type=MESH,
        )
        copy.start()
        y_copies.append(copy)
    for n, step in enumerate((0, 3, 1, 2)):
        cols = pl.ds(pl.multiple_of(lax.rem(chip + step, 4) * 256, 256), 256)
        y_copies[n].wait_recv()
        y_ref[:, cols] = (resid[here, cols] + part[here, cols] + y_in[n].astype(F32)).astype(BF16)

    pltpu.make_async_copy(lab_mid.at[three], lab_mid.at[three], a2a_sem.at[0]).wait()
    pltpu.make_async_copy(send.at[three], send.at[three], a2a_sem.at[2]).wait()
    pltpu.make_async_copy(lab_in.at[others], lab_in.at[others], a2a_sem.at[6]).wait()
    pltpu.make_async_copy(recv.at[others], recv.at[others], a2a_sem.at[9]).wait()
    for leg in range(3):
        for k in range(chunks):
            sent(k, leg)
    for copy in shipped:
        copy.wait_send()
    for copy in att_copies + y_copies:
        copy.wait_send()


def shards(chunks, patch_tokens, keep_mask, slot_index, tile_map, qkv_proj, out_proj, up_proj, down_proj):
    n_seq = lax.axis_size("seq")
    freq = jnp.asarray((10000.0 ** (-np.arange(QUART) / QUART)).astype(np.float32)).reshape(1, QUART)
    qkv = jnp.transpose(qkv_proj, (1, 2, 0, 3)).reshape(3, D, HALF)
    hbm = pl.BlockSpec(memory_space=pltpu.HBM)
    vmem = pl.BlockSpec(memory_space=pltpu.VMEM)
    y = pl.pallas_call(
        functools.partial(kernel, n_seq, chunks),
        name="encoder_layer",
        out_shape=pltpu.VMEM((64, D), BF16),
        in_specs=[hbm] * 9,
        out_specs=vmem,
        scratch_shapes=[
            pltpu.SMEM((1, 16), jnp.int32),
            pltpu.VMEM((1, 256), jnp.int32),
            pltpu.VMEM((1, 256), jnp.int32),
            pltpu.VMEM((1, QUART), F32),
            pltpu.VMEM((256, HALF), BF16),
            pltpu.VMEM((3, D, HALF), BF16),
            pltpu.VMEM((D, D), BF16),
            pltpu.VMEM((D, 2048), BF16),
            pltpu.VMEM((D, 2048), BF16),
            pltpu.VMEM((2, 256, QUART), BF16),
            pltpu.VMEM((4, n_seq // 4, 8, QUART), BF16),
            pltpu.VMEM((4, n_seq // 4, 8, QUART), BF16),
            pltpu.VMEM((n_seq // 4, 4, 8, QUART), BF16),
            pltpu.VMEM((1, 128), F32),
            pltpu.VMEM((4, 1, 128), F32),
            pltpu.VMEM((n_seq // 4, 4, 1, 128), F32),
            pltpu.VMEM((2, 2, 128, HALF), BF16),
            pltpu.VMEM((128, D), BF16),
            pltpu.VMEM((128, HALF), BF16),
            pltpu.VMEM((256, HALF), BF16),
            pltpu.VMEM((256, HALF), BF16),
            pltpu.VMEM((2, 4, 128, 128), BF16),
            pltpu.VMEM((128, D), F32),
            pltpu.VMEM((128, D), BF16),
            pltpu.VMEM((128, 2048), BF16),
            pltpu.VMEM((128, D), F32),
            pltpu.VMEM((4, 64, 256), BF16),
            pltpu.VMEM((4, 64, 256), BF16),
            pltpu.SemaphoreType.REGULAR,
            pltpu.SemaphoreType.DMA((9,)),
            pltpu.SemaphoreType.DMA((11,)),
            pltpu.SemaphoreType.DMA((4,)),
            pltpu.SemaphoreType.DMA((3 * chunks,)),
            pltpu.SemaphoreType.DMA((3 * chunks,)),
            pltpu.SemaphoreType.DMA((18,)),
            pltpu.SemaphoreType.DMA((18,)),
            pltpu.SemaphoreType.DMA((8,)),
            pltpu.SemaphoreType.DMA((4,)),
            pltpu.SemaphoreType.DMA((4,)),
        ],
        compiler_params=pltpu.CompilerParams(
            collective_id=0, has_side_effects=True, vmem_limit_bytes=58 * 1024 * 1024
        ),
    )(*[
        pltpu.with_memory_space_constraint(operand, pltpu.HBM)
        for operand in (tile_map, keep_mask, slot_index, freq, patch_tokens, qkv, out_proj, up_proj, down_proj)
    ])
    return y[None]


def solution(mesh):
    placed = (
        P("fsdp", "seq", None),
        P("fsdp", "seq"),
        P("fsdp", "seq"),
        P("fsdp", "seq"),
        P(None, "canvas", None, None),
        P(),
        P("fsdp", "canvas"),
        P("fsdp", "canvas"),
    )
    return jax.shard_map(
        functools.partial(shards, 4),
        mesh=mesh,
        in_specs=placed,
        out_specs=P("fsdp", ("seq", "canvas"), None),
        check_vma=False,
    )
```
